32 devices in a mesh: slab: 8 (over z, x), depth: 4 (over y, core).
Axes of the slice: x: 2, y: 2, z: 4, core: 2. Of those that a mesh axis runs over, the one named last changes fastest.
Arguments:
- alpha: float32 [128, 256, 512], P('slab', 'depth'), may hold values from 0 to 1
- vel_x: float32 [128, 256, 512], P('slab', 'depth'), may hold values from -1 to 1
- vel_z: float32 [128, 256, 512], P('slab', 'depth'), may hold values from -1 to 1
- divergence: float32 [128, 256, 512], P('slab', 'depth'), may hold values from -6 to 6
- press_guess: float32 [128, 256, 512], P('slab', 'depth'), may hold values from -6 to 6
- panel_records: bfloat16 [8192, 128], P(('slab', 'depth')), may hold values from -6 to 6
- panel_dest: int32 [8192, 1], P(('slab', 'depth')), may hold values from 0 to 31; in each aligned block of 256 rows (0 to 255, 256 to 511, ...) at most 16 rows name the same one
- panel_segment: int32 [8192, 1], P(('slab', 'depth')), may hold values from 0 to 4095
Outputs:
- pressure: float32 [128, 256, 512], P('slab', 'depth')
- alpha_next: float32 [128, 256, 512], P('slab', 'depth')
- panel_pressure: bfloat16 [8192, 128], P(('slab', 'depth'))
The draws below stay inside these ranges and needn't reach their ends.
Inputs may be any that keep to these rules, and one draw needn't show every extreme that they name: `panel_dest`: among the 256 panels of one device no fluid device is named more than 16 times.
All inputs are finite; a program needn't handle non-finite values.
Results may differ from the reference program's by a relative error of at most 0.001.
Values may be sent and summed in bfloat16 or wider, within the bound.
No kernel may reach another device: no remote copies, remote signals or barrier semaphores. Data moves between devices by JAX's collectives and lax.ppermute only.
A program may use at most 64 MiB of HBM per device.

```python
import math
import jax
import jax.numpy as jnp
import numpy as np

CX = 16
CZ = 64
NY = 512
PAN_DEV = 256
MORTAR = 128
NX = 128
NZ = 256
PANELS = 8192
CAP = 16
N_DEPTH = 4
DEVICES = 32


def touch_ends(result, rng, low, largest):
    extent = result.shape
    spot = [jax.random.randint(jax.random.fold_in(rng, axis), (), 0, extent[axis]) for axis in range(len(extent))]
    result = result.at[tuple(spot)].set(low)
    longest = extent.index(max(extent))
    spot[longest] = (spot[longest] + 1) % extent[longest]
    return result.at[tuple(spot)].set(largest)


def block_levels(stream_key, shape, split, low, top_value):
    factor_of, own = 1.0, jax.random.fold_in(stream_key, 6)
    for dim, shards_of in split:
        steps = jnp.exp(jax.random.uniform(jax.random.fold_in(own, dim), (shards_of,), jnp.float32, low / len(split), top_value / len(split)))
        factor_of = factor_of * jnp.repeat(steps, shape[dim] // shards_of).reshape([-1 if axis == dim else 1 for axis in range(len(shape))])
    return factor_of


def routed_block(rng, own, number, rows, amount, top, limit, slope):
    order = jax.random.permutation(rng, amount)
    packed, usual = portions_of(amount, rows * top, limit, slope, True), portions_of(amount, rows * top, limit, slope, False)
    places = jnp.arange(amount)

    def named(tallies, rotation):
        used = int((tallies > 0).sum())
        fixed = max(1, used // 4)
        passed = fixed + (places - fixed + rotation * (used - fixed)) % max(1, amount - fixed)
        return jnp.zeros((amount,), jnp.int32).at[order[jnp.where(places < fixed, places, passed)]].set(jnp.asarray(tallies, jnp.int32))

    tallies = jnp.where(number % 4 == 0, named(packed, number // 4), named(usual, number - number // 4 - 1))
    mixed = jax.random.permutation(jax.random.fold_in(own, 3), amount)
    donor, sink = mixed[0:amount // 2 * 2:2], mixed[1:amount // 2 * 2:2]
    margin = jnp.minimum(tallies[donor] - 1, limit - tallies[sink]) // 2
    margin = jnp.where((donor == order[0]) | (sink == order[0]) | (tallies[sink] == 0), 0, jnp.maximum(margin, 0))
    passed = jax.random.randint(jax.random.fold_in(own, 4), (amount // 2,), 0, 1 << 20) % (margin + 1)
    tallies = tallies.at[donor].add(-passed).at[sink].add(passed)
    items = jnp.searchsorted(jnp.cumsum(tallies), jnp.arange(rows * top), side="right").astype(jnp.int32)
    table = items.reshape(top, rows).T
    table = table[jax.random.permutation(jax.random.fold_in(own, 1), rows)]
    rotation = jax.random.randint(jax.random.fold_in(own, 2), (rows, 1), 0, top)
    return jnp.take_along_axis(table, (jnp.arange(top)[None, :] + rotation) % top, axis=1)


def portions_of(number_of, total, limit, slope, full):
    portions = [(1 << 20) // math.isqrt(standing ** slope) + 1 for standing in range(1, number_of + 1)]
    largest = limit if full else min(limit, max(-(-total // number_of), total * portions[0] // sum(portions)))
    least = 1 if total - largest >= number_of - 1 else 0
    given, surplus = [largest] + [least] * (number_of - 1), total - largest - least * (number_of - 1)
    while surplus > 0:
        free = [i for i in range(1, number_of) if given[i] < largest] or [i for i in range(1, number_of) if given[i] < limit]
        whole, budget = sum([portions[i] for i in free]), surplus
        for i in free:
            more = min(limit - given[i], max(1, budget * portions[i] // whole), surplus)
            given[i] = given[i] + more
            surplus = surplus - more
    return np.array(given)


def scatter_about(stream_key, shape, spread, bound, pieces=(), held_as=jnp.bfloat16):
    entries = jax.random.normal(stream_key, shape, jnp.float32) * spread
    if len(pieces) > 0:
        entries = block_levels(stream_key, shape, pieces, -0.22, 0.18) * entries
    return jnp.clip(entries, min=-bound, max=bound).astype(held_as)


def setup_inputs(seed: int = 0) -> dict:
    seeds = jax.random.split(jax.random.key(seed), 9)
    alpha = jnp.clip(1.0 * jax.random.uniform(seeds[0], (NX, NZ, NY), jnp.float32) ** block_levels(seeds[0], (NX, NZ, NY), ((0, 8), (1, 4)), -0.2, 0.2), 0.0, 1.0)
    vel_x = jnp.clip(jax.random.uniform(seeds[1], (NX, NZ, NY), jnp.float32, -1.0, 1.0) * block_levels(seeds[1], (NX, NZ, NY), ((0, 8), (1, 4)), -0.4, 0.0), -1.0, 1.0)
    vel_z = jnp.clip(jax.random.uniform(seeds[2], (NX, NZ, NY), jnp.float32, -1.0, 1.0) * block_levels(seeds[2], (NX, NZ, NY), ((0, 8), (1, 4)), -0.4, 0.0), -1.0, 1.0)
    divergence = scatter_about(seeds[3], (NX, NZ, NY), 1.0, 6.0, ((0, 8), (1, 4)), jnp.float32)
    press_guess = scatter_about(seeds[4], (NX, NZ, NY), 1.0, 6.0, ((0, 8), (1, 4)), jnp.float32)
    panel_records = scatter_about(seeds[5], (PANELS, MORTAR), 1.0, 6.0, ((0, 32),))
    panel_dest_keys = jax.random.split(jax.random.fold_in(seeds[6], 1), PANELS // PAN_DEV)
    panel_dest_turns = jax.random.permutation(jax.random.fold_in(seeds[6], 3), PANELS // PAN_DEV)
    panel_dest = jax.vmap(lambda own, number: routed_block(jax.random.fold_in(seeds[6], 2), own, number, PAN_DEV, DEVICES, 1, CAP, 2))(panel_dest_keys, panel_dest_turns).reshape((PANELS, 1))
    panel_segment = touch_ends(jax.random.randint(seeds[7], (PANELS, 1), 0, CX * CZ * NY // 128), jax.random.fold_in(seeds[7], 1), 0, (CX * CZ * NY // 128) - 1).astype(jnp.int32)
    return {"alpha": alpha, "vel_x": vel_x, "vel_z": vel_z, "divergence": divergence, "press_guess": press_guess, "panel_records": panel_records, "panel_dest": panel_dest, "panel_segment": panel_segment}


COURANT = 0.2


def advect_core(alpha_pad, velx_pad, velz_pad):
    face_x = velx_pad[1:, 1:-1] * jnp.where(velx_pad[1:, 1:-1] > 0, alpha_pad[:-1, 1:-1], alpha_pad[1:, 1:-1])
    face_z = velz_pad[1:-1, 1:] * jnp.where(velz_pad[1:-1, 1:] > 0, alpha_pad[1:-1, :-1], alpha_pad[1:-1, 1:])
    change = face_x[1:] - face_x[:-1] + face_z[:, 1:] - face_z[:, :-1]
    return alpha_pad[1:-1, 1:-1] - COURANT * change


def sweep(press_pad, dens_pad, rhs):
    press_pad = jnp.pad(press_pad, ((0, 0), (0, 0), (1, 1)))
    dens_pad = jnp.pad(dens_pad, ((0, 0), (0, 0), (1, 1)))
    rows_all = rhs.shape[0]
    cols_all = rhs.shape[1]
    beam = rhs.shape[2]
    own_rho = dens_pad[1:1 + rows_all, 1:1 + cols_all, 1:1 + beam]
    total = jnp.zeros_like(rhs)
    weight = jnp.zeros_like(rhs)
    for off_x, off_z, off_y in ((0, 1, 1), (2, 1, 1), (1, 0, 1), (1, 2, 1), (1, 1, 0), (1, 1, 2)):
        next_p = press_pad[off_x:off_x + rows_all, off_z:off_z + cols_all, off_y:off_y + beam]
        next_rho = dens_pad[off_x:off_x + rows_all, off_z:off_z + cols_all, off_y:off_y + beam]
        coeff = 2.0 / (own_rho + next_rho)
        total = total + coeff * next_p
        weight = weight + coeff
    return (total - rhs) / weight


def pad_two(field):
    return jnp.pad(field, ((1, 1), (1, 1), (0, 0)))


def reference(alpha, vel_x, vel_z, divergence, press_guess, panel_records, panel_dest, panel_segment):
    blocks = NY // 128
    target = panel_dest[:, 0]
    segment = panel_segment[:, 0]
    slab_of = target // N_DEPTH
    depth_of = target % N_DEPTH
    local_x = segment // (CZ * blocks)
    local_z = (segment // blocks) % CZ
    block_y = segment % blocks
    global_row = ((slab_of * CX + local_x) * NZ + depth_of * CZ + local_z) * blocks + block_y
    global_row = global_row.astype(jnp.int32)
    hull = jnp.zeros((NX * NZ * blocks, 128), jnp.float32).at[global_row].add(panel_records.astype(jnp.float32))
    hull = hull.reshape(NX, NZ, NY)
    alpha_next = advect_core(pad_two(alpha), pad_two(vel_x), pad_two(vel_z))
    density = 1.0 + 9.0 * alpha_next
    rhs = divergence + hull
    dens_pad = pad_two(density)
    pressure = press_guess
    for sweep_number in range(3):
        pressure = sweep(pad_two(pressure), dens_pad, rhs)
    panel_pressure = pressure.reshape(-1, 128).astype(jnp.bfloat16)[global_row]
    return pressure, alpha_next, panel_pressure
```

```python
import functools

import jax
import jax.numpy as jnp
from jax import lax
from jax.experimental import pallas as pl
from jax.experimental.pallas import tpu as pltpu
from jax.sharding import PartitionSpec as P

COURANT = 0.2
LANES = 128
SUB = 8
DIGIT = 256
MIB = 1 << 20
F32 = jnp.float32
BF16 = jnp.bfloat16

WHOLE = pl.BlockSpec(memory_space=pltpu.VMEM)
FAR = pl.BlockSpec(memory_space=pltpu.HBM)
DMA = pltpu.SemaphoreType.DMA


def call(kernel, outs, *args, aliases=None, far_in=(), far_out=(), in_specs=None, scratch=(), limit=12 * MIB, name=None):
    specs = [FAR if n in far_in else WHOLE for n in range(len(args))]
    for n, spec in (in_specs or {}).items():
        specs[n] = spec
    shapes = [o if n in far_out else pltpu.VMEM(o.shape, o.dtype) for n, o in enumerate(outs)]
    return pl.pallas_call(
        kernel,
        out_shape=shapes,
        in_specs=specs,
        out_specs=[FAR if n in far_out else WHOLE for n in range(len(outs))],
        scratch_shapes=list(scratch),
        input_output_aliases=aliases or {},
        compiler_params=pltpu.CompilerParams(vmem_limit_bytes=limit),
        name=name,
    )(*(pltpu.with_memory_space_constraint(a, pltpu.HBM) if n in far_in else a for n, a in enumerate(args)))


def shape(dims, dtype=F32):
    return jax.ShapeDtypeStruct(tuple(dims), dtype)


def even(axis):
    return lax.rem(lax.axis_index(axis), 2) == 0


def swap(block, axis, odd):
    count = lax.axis_size(axis)
    pairs = []
    for i in range(odd, count - 1, 2):
        pairs += [(i, i + 1), (i + 1, i)]
    if not pairs:
        return jnp.zeros_like(block)
    return lax.ppermute(block, axis, pairs)


def row_is(rows, index):
    return lax.broadcasted_iota(jnp.int32, rows, 0) == index


def z_tiles(ref):
    last = ref.shape[1] // SUB - 1
    return [ref.at[:, pl.ds(0, SUB), :], ref.at[:, pl.ds(last * SUB, SUB), :]]


def x_planes(ref):
    return [ref.at[0], ref.at[ref.shape[0] - 1]]


def fetch(sources, targets, sems):
    copies = []
    for n, (source, target) in enumerate(zip(sources, targets)):
        copies.append(pltpu.make_async_copy(source, target, sems.at[n]))
        copies[-1].start()
    return copies


def pack_first(alpha, vx, vz, xe, xo, ze, zo, a0, a1, az0, az1, vx0, vz0, sems):
    sources = x_planes(alpha) + z_tiles(alpha) + x_planes(vx)[:1] + z_tiles(vz)[:1]
    for copy in fetch(sources, [a0, a1, az0, az1, vx0, vz0], sems):
        copy.wait()
    ev_x = even("slab")
    ev_z = even("depth")

    def fold(v, a):
        return jnp.where(v > 0, v, v * a)

    for k in range(a0.shape[0] // SUB):
        at = pl.ds(k * SUB, SUB)
        up = a1[at, :]
        down = fold(vx0[at, :], a0[at, :])
        xe[at, :] = jnp.where(ev_x, up, down).astype(BF16)
        xo[at, :] = jnp.where(ev_x, down, up).astype(BF16)
    for x in range(az0.shape[0]):
        up = az1[x, SUB - 1:SUB, :]
        down = fold(vz0[x, 0:1, :], az0[x, 0:1, :])
        ze[x:x + 1, :] = jnp.where(ev_z, up, down)
        zo[x:x + 1, :] = jnp.where(ev_z, down, up)


def route(capacity, rows, devices, dest, seg, rec, send, slot_out):
    panels = dest.shape[1]
    d = dest[...]
    s = seg[...]
    hot = lax.broadcasted_iota(jnp.int32, (devices, panels), 0) == d
    hot_f = jnp.where(hot, 1.0, 0.0)
    before_me = lax.broadcasted_iota(jnp.int32, (panels, panels), 0) < lax.broadcasted_iota(
        jnp.int32, (panels, panels), 1
    )
    before = jnp.dot(
        hot_f.astype(BF16), jnp.where(before_me, 1.0, 0.0).astype(BF16), preferred_element_type=F32
    )
    slot = jnp.sum(before * hot_f, axis=0, keepdims=True).astype(jnp.int32)
    place = d * rows + slot
    pick = lax.broadcasted_iota(jnp.int32, (devices * rows, panels), 0) == place
    records = jnp.dot(jnp.where(pick, 1.0, 0.0).astype(BF16), rec[...], preferred_element_type=F32)
    high = (s // DIGIT).astype(F32)
    low = (s % DIGIT).astype(F32)
    lane = lax.broadcasted_iota(jnp.int32, (LANES, panels), 0)
    at_high = jnp.where(lane == slot, 1.0, 0.0).astype(BF16)
    at_low = jnp.where(lane == slot + capacity, 1.0, 0.0).astype(BF16)
    contract = (((1,), (1,)), ((), ()))
    digits = lax.dot_general(
        (hot_f * high).astype(BF16), at_high, contract, preferred_element_type=F32
    ) + lax.dot_general((hot_f * low).astype(BF16), at_low, contract, preferred_element_type=F32)
    records = records.reshape(devices, rows, LANES)
    is_digit = lax.broadcasted_iota(jnp.int32, records.shape, 1) >= capacity
    send[...] = jnp.where(is_digit, digits[:, None, :], records).astype(BF16)
    slot_out[...] = d * capacity + slot


def parts_of(cells_x):
    step = max(1, cells_x // 4)
    return [(first, min(step, cells_x - first)) for first in range(0, cells_x, step)]


def fetch_field(source, target, sems, row):
    copies = []
    for n, (first, count) in enumerate(parts_of(target.shape[0])):
        planes = pl.ds(first, count)
        copies.append(pltpu.make_async_copy(source.at[planes], target.at[planes], sems.at[row, n]))
        copies[-1].start()
    return copies


def advect(
    alpha_h, vx_h, vz_h, p_h, xe_in, xo_in, ze_in, zo_in,
    out_h, xe, xo, ze, zo,
    alpha, vx, vz, out, p0, p1, pz0, pz1, sems, p_sems,
):
    cells_x, cells_z, beam = alpha.shape
    chunks = cells_z // SUB
    ev_x = even("slab")
    ev_z = even("depth")
    top = row_is((SUB, beam), 0)
    bottom = row_is((SUB, beam), SUB - 1)
    parts = parts_of(cells_x)
    ins = [fetch_field(h, v, sems, n) for n, (h, v) in enumerate(((alpha_h, alpha), (vx_h, vx), (vz_h, vz)))]
    p_ins = fetch(x_planes(p_h) + z_tiles(p_h), [p0, p1, pz0, pz1], p_sems)
    outs = [
        pltpu.make_async_copy(out.at[pl.ds(f, c)], out_h.at[pl.ds(f, c)], sems.at[len(ins), n])
        for n, (f, c) in enumerate(parts)
    ]

    def at(k):
        return pl.ds(k * SUB, SUB)

    def plane(x, first, last):
        zlo = jnp.where(ev_z, zo_in[pl.ds(x, 1), :], ze_in[pl.ds(x, 1), :])
        zhi = jnp.where(ev_z, ze_in[pl.ds(x, 1), :], zo_in[pl.ds(x, 1), :])
        above = None
        for k in reversed(range(chunks)):
            a = alpha[x, at(k), :]
            v = vx[x, at(k), :]
            if first:
                am = jnp.where(ev_x, xo_in[at(k), :], xe_in[at(k), :]).astype(F32)
            else:
                am = alpha[x - 1, at(k), :]
            fx = v * jnp.where(v > 0, am, a)
            if last:
                q = jnp.where(ev_x, xe_in[at(k), :], xo_in[at(k), :]).astype(F32)
                fxn = jnp.where(q > 0, q * a, q)
            else:
                vn = vx[x + 1, at(k), :]
                fxn = vn * jnp.where(vn > 0, a, alpha[x + 1, at(k), :])
            w = vz[x, at(k), :]
            if k == 0:
                edge = jnp.broadcast_to(zlo, a.shape)
            else:
                edge = pltpu.roll(alpha[x, at(k - 1), :], 1, 0)
            ad = jnp.where(top, edge, pltpu.roll(a, 1, 0))
            fz = w * jnp.where(w > 0, ad, a)
            up = pltpu.roll(fz, SUB - 1, 0)
            if above is None:
                q = jnp.broadcast_to(zhi, a.shape)
                fzn = jnp.where(bottom, jnp.where(q > 0, q * a, q), up)
            else:
                fzn = jnp.where(bottom, above, up)
            above = up
            new = a - COURANT * (fxn - fx + fzn - fz)
            out[x, at(k), :] = new
            if k == chunks - 1:
                z_up = new[SUB - 1:SUB, :] - 0.5
            if k == 0:
                z_down = new[0:1, :] - 0.5
        ze[0, pl.ds(x, 1), :] = jnp.where(ev_z, z_up, z_down)
        zo[0, pl.ds(x, 1), :] = jnp.where(ev_z, z_down, z_up)

    for n, (first, count) in enumerate(parts):
        for copies in ins:
            copies[n].wait()
        begin = max(first - 1, 0)
        end = first + count - 1
        if begin == 0:
            plane(0, True, end == begin and cells_x == 1)
            begin = 1

        @pl.loop(begin, end)
        def _(x):
            plane(x, False, False)

        if n == len(parts) - 1:
            plane(cells_x - 1, False, True)
        if n > 0:
            outs[n - 1].start()
    outs[-1].start()

    for copy in p_ins:
        copy.wait()
    for k in range(chunks):
        for which, up, down in ((0, out[cells_x - 1, at(k), :] - 0.5, out[0, at(k), :] - 0.5), (1, p1[at(k), :], p0[at(k), :])):
            xe[which, at(k), :] = jnp.where(ev_x, up, down).astype(BF16)
            xo[which, at(k), :] = jnp.where(ev_x, down, up).astype(BF16)
    for x in range(cells_x):
        up = pz1[x, SUB - 1:SUB, :]
        down = pz0[x, 0:1, :]
        ze[1, x:x + 1, :] = jnp.where(ev_z, up, down)
        zo[1, x:x + 1, :] = jnp.where(ev_z, down, up)
    for copy in outs:
        copy.wait()


def coefficients(alpha_h, after, alpha, cx, cz, cy, inverse, sems):
    del after
    cells_x, cells_z, beam = alpha.shape
    chunks = cells_z // SUB
    top = row_is((SUB, beam), 0)
    bottom = row_is((SUB, beam), SUB - 1)
    lane = lax.broadcasted_iota(jnp.int32, (SUB, beam), 1)
    ins = fetch_field(alpha_h, alpha, sems, 0)
    cx[0] = jnp.zeros((cells_z, beam), F32)

    def at(k):
        return pl.ds(k * SUB, SUB)

    def plane(x):
        inside = jnp.where(x < cells_x - 1, 2.0, 0.0)
        nxt = jnp.minimum(x + 1, cells_x - 1)
        above = jnp.zeros((SUB, beam), F32)
        for k in reversed(range(chunks)):
            rho = 1.0 + 9.0 * alpha[x, at(k), :]
            rho_x = 1.0 + 9.0 * alpha[nxt, at(k), :]
            hx = inside / (rho + rho_x)
            cx[x + 1, at(k), :] = hx
            rolled = pltpu.roll(rho, 1, 0)
            if k == 0:
                hz = jnp.where(top, 0.0, 2.0 / (rho + rolled))
            else:
                below = pltpu.roll(1.0 + 9.0 * alpha[x, at(k - 1), :], 1, 0)
                hz = 2.0 / (rho + jnp.where(top, below, rolled))
            cz[x, at(k), :] = hz
            up = pltpu.roll(hz, SUB - 1, 0)
            hz_up = jnp.where(bottom, above, up)
            above = up
            hy_all = 2.0 / (rho + jnp.where(lane == 0, 0.0, pltpu.roll(rho, 1, 1)))
            hy = jnp.where(lane == 0, 0.0, hy_all)
            cy[x, at(k), :] = hy
            far = rho[:, beam - LANES:]
            edge = jnp.where(lane[:, beam - LANES:] == beam - 1, 2.0 / far, 0.0)
            hy_up = pltpu.roll(hy, beam - 1, 1)
            hy_up = jnp.concatenate(
                [hy_up[:, : beam - LANES], hy_up[:, beam - LANES:] + edge], axis=1
            )
            inverse[x, at(k), :] = 1.0 / (cx[x, at(k), :] + hx + hz + hz_up + hy_all + hy_up)

    parts = parts_of(cells_x)
    for n, (first, count) in enumerate(parts):
        ins[n].wait()
        end = cells_x if n == len(parts) - 1 else first + count - 1

        @pl.loop(max(first - 1, 0), end)
        def _(x):
            plane(x)


def close(
    p_in, inverse_in, alpha, xe_in, xo_in, ze_in, zo_in,
    p, inverse, gx, gz, xe, xo, ze, zo,
    wx,
):
    del p_in, inverse_in
    cells_x, cells_z, beam = alpha.shape
    chunks = cells_z // SUB
    i, j = lax.axis_index("slab"), lax.axis_index("depth")
    ev_x, ev_z = even("slab"), even("depth")
    has = [
        [jnp.where(i > 0, 1.0, 0.0), jnp.where(i < lax.axis_size("slab") - 1, 1.0, 0.0)],
        [jnp.where(j > 0, 1.0, 0.0), jnp.where(j < lax.axis_size("depth") - 1, 1.0, 0.0)],
    ]

    def at(k):
        return pl.ds(k * SUB, SUB)

    for side, x in ((0, 0), (1, cells_x - 1)):
        for k in range(chunks):
            a, b = xe_in[:, at(k), :], xo_in[:, at(k), :]
            v = (jnp.where(ev_x, a, b) if side else jnp.where(ev_x, b, a)).astype(F32)
            halo = has[0][side] * (9.0 * v[0] + 5.5)
            c = 2.0 / (1.0 + 9.0 * alpha[x, at(k), :] + halo)
            w = 1.0 / inverse[x, at(k), :]
            p[x, at(k), :] = p[x, at(k), :] * w + c * v[1]
            gx[side, at(k), :] = c
            wx[side, at(k), :] = w + c

    def rows(x, plane):
        faces = []
        for side, k in ((0, 0), (1, chunks - 1)):
            here = row_is((SUB, beam), 0 if side == 0 else SUB - 1)
            a, b = ze_in[:, pl.ds(x, 1), :], zo_in[:, pl.ds(x, 1), :]
            v = jnp.where(ev_z, a, b) if side else jnp.where(ev_z, b, a)
            halo = jnp.broadcast_to(has[1][side] * (9.0 * v[0] + 5.5), (SUB, beam))
            c = jnp.where(here, 2.0 / (1.0 + 9.0 * alpha[x, at(k), :] + halo), 0.0)
            add = c * jnp.broadcast_to(v[1], (SUB, beam))
            if plane is None:
                w = 1.0 / inverse[x, at(k), :]
                total = p[x, at(k), :] * w + add
                inv = 1.0 / (w + c)
                inverse[x, at(k), :] = inv
                new = total * inv
                p[x, at(k), :] = new
            else:
                w = wx[plane, at(k), :] + c
                wx[plane, at(k), :] = w
                inv = 1.0 / w
                total = p[x, at(k), :] + add
                p[x, at(k), :] = total
                new = total * inv
            g = inv * c
            r = slice(0, 1) if side == 0 else slice(SUB - 1, SUB)
            gz[side, pl.ds(x, 1), :] = g[r, :]
            faces.append(new[r, :])
        ze[pl.ds(x, 1), :] = jnp.where(ev_z, faces[1], faces[0])
        zo[pl.ds(x, 1), :] = jnp.where(ev_z, faces[0], faces[1])

    rows(0, 0)
    rows(cells_x - 1, 1)

    @pl.loop(1, cells_x - 1)
    def _(x):
        rows(x, None)

    for k in range(chunks):
        new = []
        for side, x in ((0, 0), (1, cells_x - 1)):
            inv = 1.0 / wx[side, at(k), :]
            inverse[x, at(k), :] = inv
            gx[side, at(k), :] = gx[side, at(k), :] * inv
            new.append(p[x, at(k), :] * inv)
            p[x, at(k), :] = new[side]
        xe[at(k), :] = jnp.where(ev_x, new[1], new[0]).astype(BF16)
        xo[at(k), :] = jnp.where(ev_x, new[0], new[1]).astype(BF16)


def by_lanes(ref):
    cells_x, cells_z, beam = ref.shape
    blocks = beam // LANES
    for b in range(blocks):
        yield b, pl.ds(b * LANES, LANES)


def scatter(capacity, got, div_h, rhs, row_out, rec32, row_v, row_s, hull, div, sems, sem):
    devices, rows, _ = got.shape
    cells_x, cells_z, beam = rhs.shape
    blocks = beam // LANES
    ins = fetch_field(div_h, div, sems, 0)
    digits = got[:, rows - 1, :].astype(F32)
    seg = (digits * float(DIGIT) + pltpu.roll(digits, LANES - capacity, 1)).astype(jnp.int32)
    across = seg // blocks
    row = ((across // cells_z) * blocks + seg % blocks) * cells_z + across % cells_z
    row_v[...] = row
    row_out[...] = row
    copy = pltpu.make_async_copy(row_v, row_s, sem)
    copy.start()
    rec32[...] = got[...].astype(F32).reshape(devices * rows, LANES)
    hull[...] = jnp.zeros_like(hull)
    copy.wait()

    @pl.loop(0, devices)
    def _(d):
        for s in range(capacity):
            n = row_s[d, s]
            hull[pl.ds(n, 1), :] += rec32[pl.ds(d * rows + s, 1), :]

    for copy in ins:
        copy.wait()

    @pl.loop(0, cells_x)
    def _(x):
        for b, lanes in by_lanes(rhs):
            first = pl.multiple_of((x * blocks + b) * cells_z, SUB)
            rhs[x, :, lanes] = div[x, :, lanes] + hull[pl.ds(first, cells_z), :]


def sweep(p, cx, cz, cy, inverse, rhs, out):
    cells_x, cells_z, beam = p.shape
    chunks = cells_z // SUB
    top = row_is((SUB, beam), 0)
    bottom = row_is((SUB, beam), SUB - 1)

    def at(k):
        return pl.ds(k * SUB, SUB)

    @pl.loop(0, cells_x)
    def _(x):
        prv = jnp.maximum(x - 1, 0)
        nxt = jnp.minimum(x + 1, cells_x - 1)
        above = jnp.zeros((SUB, beam), F32)
        rolled = pltpu.roll(p[x, at(chunks - 1), :], 1, 0)
        for k in reversed(range(chunks)):
            here = p[x, at(k), :]
            hz = cz[x, at(k), :]
            hy = cy[x, at(k), :]
            total = cx[x, at(k), :] * p[prv, at(k), :] + cx[x + 1, at(k), :] * p[nxt, at(k), :]
            if k > 0:
                below = pltpu.roll(p[x, at(k - 1), :], 1, 0)
                down = jnp.where(top, below, rolled)
                rolled = below
            else:
                down = rolled
            up = pltpu.roll(hz * here, SUB - 1, 0)
            total = total + (hz * down + jnp.where(bottom, above, up))
            above = up
            total = total + (hy * pltpu.roll(here, 1, 1) + pltpu.roll(hy * here, beam - 1, 1))
            out[x, at(k), :] = (total - rhs[x, at(k), :]) * inverse[x, at(k), :]


def add_borders(p_in, xe_in, xo_in, ze_in, zo_in, gx, gz, p, send=None):
    del p_in
    cells_x, cells_z, beam = p.shape
    chunks = cells_z // SUB
    ev_x, ev_z = even("slab"), even("depth")

    def at(k):
        return pl.ds(k * SUB, SUB)

    for side, x in ((0, 0), (1, cells_x - 1)):
        for k in range(chunks):
            a, b = xe_in[at(k), :], xo_in[at(k), :]
            v = jnp.where(ev_x, a, b) if side else jnp.where(ev_x, b, a)
            p[x, at(k), :] = p[x, at(k), :] + gx[side, at(k), :] * v.astype(F32)

    @pl.loop(0, cells_x)
    def _(x):
        faces = []
        for side, k in ((0, 0), (1, chunks - 1)):
            here = row_is((SUB, beam), 0 if side == 0 else SUB - 1)
            a, b = ze_in[pl.ds(x, 1), :], zo_in[pl.ds(x, 1), :]
            v = jnp.where(ev_z, a, b) if side else jnp.where(ev_z, b, a)
            add = jnp.broadcast_to(gz[side, pl.ds(x, 1), :] * v, (SUB, beam))
            new = p[x, at(k), :] + jnp.where(here, add, 0.0)
            p[x, at(k), :] = new
            faces.append(new[0:1, :] if side == 0 else new[SUB - 1:SUB, :])
        if send is not None:
            send[2][pl.ds(x, 1), :] = jnp.where(ev_z, faces[1], faces[0])
            send[3][pl.ds(x, 1), :] = jnp.where(ev_z, faces[0], faces[1])

    if send is not None:
        for k in range(chunks):
            lo, hi = p[0, at(k), :], p[cells_x - 1, at(k), :]
            send[0][at(k), :] = jnp.where(ev_x, hi, lo).astype(BF16)
            send[1][at(k), :] = jnp.where(ev_x, lo, hi).astype(BF16)


def fix_and_send(p_in, xe_in, xo_in, ze_in, zo_in, gx, gz, p, xe, xo, ze, zo):
    add_borders(p_in, xe_in, xo_in, ze_in, zo_in, gx, gz, p, (xe, xo, ze, zo))


def fix_and_gather(
    capacity, p_in, xe_in, xo_in, ze_in, zo_in, gx, gz, row, p_h, back, p, split, rows32, sems
):
    cells_x, cells_z, beam = p.shape
    p[...] = p_in[...]
    add_borders(p_in, xe_in, xo_in, ze_in, zo_in, gx, gz, p)
    blocks = beam // LANES
    devices = back.shape[0]
    out = pltpu.make_async_copy(p, p_h, sems)
    out.start()

    @pl.loop(0, cells_x)
    def _(x):
        for b, lanes in by_lanes(p):
            first = pl.multiple_of((x * blocks + b) * cells_z, SUB)
            split[pl.ds(first, cells_z), :] = p[x, :, lanes]

    @pl.loop(0, devices)
    def _(d):
        for s in range(capacity):
            rows32[pl.ds(d * capacity + s, 1), :] = split[pl.ds(row[d, s], 1), :]

    back[...] = rows32[...].astype(BF16).reshape(back.shape)
    out.wait()


def unroute(back, slot, out):
    rows = back.shape[0] * back.shape[1]
    panels = out.shape[0]
    pick = lax.broadcasted_iota(jnp.int32, (rows, panels), 0) == slot[...]
    out[...] = lax.dot_general(
        jnp.where(pick, 1.0, 0.0).astype(BF16),
        back[...].reshape(rows, LANES),
        (((0,), (0,)), ((), ())),
        preferred_element_type=F32,
    ).astype(BF16)


def body(alpha, vel_x, vel_z, divergence, press_guess, panel_records, panel_dest, panel_segment):
    devices = lax.axis_size("slab") * lax.axis_size("depth")
    panels = panel_records.shape[0]
    capacity = 2 * panels // devices
    cells_x, cells_z, beam = alpha.shape
    field = shape(alpha.shape)
    rows = -(-(capacity + 1) // SUB) * SUB
    axes = ("slab", "depth")

    xs, zs = (cells_z, beam), (cells_x, beam)
    tile = (cells_x, SUB, beam)
    faces = [shape(xs, BF16)] * 2 + [shape(zs)] * 2
    two_faces = [shape((2,) + xs, BF16)] * 2 + [shape((2,) + zs)] * 2
    parts = len(parts_of(cells_x))
    lines = (cells_x * cells_z * beam // LANES, LANES)

    def near(dims, dtype=F32):
        return pltpu.VMEM(tuple(dims), dtype)

    def swaps(xe, xo, ze, zo):
        return swap(xe, "slab", 0), swap(xo, "slab", 1), swap(ze, "depth", 0), swap(zo, "depth", 1)

    send, slot = call(
        functools.partial(route, capacity, rows, devices),
        [shape((devices, rows, LANES), BF16), shape((1, panels), jnp.int32)],
        panel_dest.reshape(1, panels), panel_segment.reshape(1, panels), panel_records,
        name="route",
    )
    got = lax.all_to_all(send, axes, split_axis=0, concat_axis=0, tiled=True)

    packed = call(
        pack_first, faces, alpha, vel_x, vel_z,
        far_in=(0, 1, 2),
        scratch=[near(xs), near(xs), near(tile), near(tile), near(xs), near(tile), DMA((6,))],
        name="pack_first",
    )
    alpha_next, *packed = call(
        advect, [field] + two_faces, alpha, vel_x, vel_z, press_guess, *swaps(*packed),
        far_in=(0, 1, 2, 3), far_out=(0,),
        scratch=[near(alpha.shape)] * 4 + [near(xs), near(xs), near(tile), near(tile), DMA((4, parts)), DMA((4,))],
        name="advect",
    )
    halo = swaps(*packed)
    near_alpha, cx, cz, cy, inverse = call(
        coefficients,
        [field, shape((cells_x + 1,) + xs), field, field, field],
        alpha_next, got,
        far_in=(0,),
        in_specs={1: pl.BlockSpec(memory_space=pl.ANY)},
        scratch=[DMA((1, parts))],
        name="coefficients",
    )
    rhs, row = call(
        functools.partial(scatter, capacity),
        [field, shape((devices, LANES), jnp.int32)],
        got, divergence,
        far_in=(1,),
        scratch=[
            near((devices * rows, LANES)),
            near((devices, LANES), jnp.int32),
            pltpu.SMEM((devices, LANES), jnp.int32),
            near(lines),
            near(alpha.shape),
            DMA((1, parts)),
            DMA,
        ],
        name="scatter",
    )
    (pressure,) = call(sweep, [field], press_guess, cx, cz, cy, inverse, rhs, name="sweep")
    pressure, inverse, gx, gz, *packed = call(
        close,
        [field, field, shape((2,) + xs), shape((2,) + zs)] + faces,
        pressure, inverse, near_alpha, *halo,
        aliases={0: 0, 1: 1},
        scratch=[near((2,) + xs)],
        name="close",
    )
    halo = swaps(*packed)
    (pressure,) = call(sweep, [field], pressure, cx, cz, cy, inverse, rhs, name="sweep")
    pressure, *packed = call(
        fix_and_send, [field] + faces, pressure, *halo, gx, gz, aliases={0: 0}, name="fix"
    )
    halo = swaps(*packed)
    (pressure,) = call(sweep, [field], pressure, cx, cz, cy, inverse, rhs, name="sweep")
    pressure, back = call(
        functools.partial(fix_and_gather, capacity),
        [field, shape((devices, capacity, LANES), BF16)],
        pressure, *halo, gx, gz, row,
        far_out=(0,),
        in_specs={7: pl.BlockSpec(memory_space=pltpu.SMEM)},
        scratch=[near(alpha.shape), near(lines), near((devices * capacity, LANES)), DMA],
        name="gather",
    )
    returned = lax.all_to_all(back, axes, split_axis=0, concat_axis=0, tiled=True)
    panel_pressure = pl.pallas_call(
        unroute,
        out_shape=shape((panels, LANES), BF16),
        in_specs=[WHOLE] * 2,
        out_specs=WHOLE,
        name="unroute",
    )(returned, slot)
    return (pressure, alpha_next, panel_pressure)


def solution(mesh):
    in_specs = (
        P("slab", "depth", None),
        P("slab", "depth", None),
        P("slab", "depth", None),
        P("slab", "depth", None),
        P("slab", "depth", None),
        P(("slab", "depth"), None),
        P(("slab", "depth"), None),
        P(("slab", "depth"), None),
    )
    out_specs = (P("slab", "depth", None), P("slab", "depth", None), P(("slab", "depth"), None))
    return jax.shard_map(body, mesh=mesh, in_specs=in_specs, out_specs=out_specs, check_vma=False)
```

```python
import functools

import jax
import jax.numpy as jnp
from jax import lax
from jax.experimental import pallas as pl
from jax.experimental.pallas import tpu as pltpu
from jax.sharding import PartitionSpec as P

COURANT = 0.2
LANES = 128
SUB = 8
DIGIT = 256
MIB = 1 << 20
F32 = jnp.float32
BF16 = jnp.bfloat16

WHOLE = pl.BlockSpec(memory_space=pltpu.VMEM)
FAR = pl.BlockSpec(memory_space=pltpu.HBM)
DMA = pltpu.SemaphoreType.DMA


def call(kernel, outs, *args, aliases=None, far_in=(), far_out=(), free_out=(), in_specs=None, scratch=(), limit=12 * MIB, name=None):
    specs = [FAR if n in far_in else WHOLE for n in range(len(args))]
    for n, spec in (in_specs or {}).items():
        specs[n] = spec
    shapes = [o if n in far_out or n in free_out else pltpu.VMEM(o.shape, o.dtype) for n, o in enumerate(outs)]
    return pl.pallas_call(
        kernel,
        out_shape=shapes,
        in_specs=specs,
        out_specs=[FAR if n in far_out else WHOLE for n in range(len(outs))],
        scratch_shapes=list(scratch),
        input_output_aliases=aliases or {},
        compiler_params=pltpu.CompilerParams(vmem_limit_bytes=limit),
        name=name,
    )(*(pltpu.with_memory_space_constraint(a, pltpu.HBM) if n in far_in else a for n, a in enumerate(args)))


def shape(dims, dtype=F32):
    return jax.ShapeDtypeStruct(tuple(dims), dtype)


def even(axis):
    return lax.rem(lax.axis_index(axis), 2) == 0


def swap(block, axis, odd):
    slabs, depths = lax.axis_size("slab"), lax.axis_size("depth")
    pairs = []
    for i in range(slabs):
        for j in range(depths):
            own, count, other = (i, slabs, depths) if axis == "slab" else (j, depths, slabs)
            partner = own + 1 if own % 2 == odd else own - 1
            target = (partner, j) if axis == "slab" else (i, partner)
            if not 0 <= partner < count:
                if other % 2:
                    continue
                target = (i, j ^ 1) if axis == "slab" else (i ^ 1, j)
            pairs.append((i * depths + j, target[0] * depths + target[1]))
    return lax.ppermute(block, ("slab", "depth"), pairs)


def inner(axis):
    i = lax.axis_index(axis)
    return [jnp.where(i > 0, 1.0, 0.0), jnp.where(i < lax.axis_size(axis) - 1, 1.0, 0.0)]


def row_is(rows, index):
    return lax.broadcasted_iota(jnp.int32, rows, 0) == index


def z_tiles(ref):
    last = ref.shape[1] // SUB - 1
    return [ref.at[:, pl.ds(0, SUB), :], ref.at[:, pl.ds(last * SUB, SUB), :]]


def x_planes(ref):
    return [ref.at[0], ref.at[ref.shape[0] - 1]]


def fetch(sources, targets, sems):
    copies = []
    for n, (source, target) in enumerate(zip(sources, targets)):
        copies.append(pltpu.make_async_copy(source, target, sems.at[n]))
        copies[-1].start()
    return copies


def pack_first(alpha, vx, vz, xe, xo, ze, zo, a0, a1, az0, az1, vx0, vz0, sems):
    sources = x_planes(alpha) + z_tiles(alpha) + x_planes(vx)[:1] + z_tiles(vz)[:1]
    for copy in fetch(sources, [a0, a1, az0, az1, vx0, vz0], sems):
        copy.wait()
    ev_x = even("slab")
    ev_z = even("depth")

    def fold(v, a):
        return jnp.where(v > 0, v, v * a)

    for k in range(a0.shape[0] // SUB):
        at = pl.ds(k * SUB, SUB)
        up = a1[at, :]
        down = fold(vx0[at, :], a0[at, :])
        xe[at, :] = jnp.where(ev_x, up, down).astype(BF16)
        xo[at, :] = jnp.where(ev_x, down, up).astype(BF16)
    for x in range(az0.shape[0]):
        up = az1[x, SUB - 1:SUB, :]
        down = fold(vz0[x, 0:1, :], az0[x, 0:1, :])
        ze[x:x + 1, :] = jnp.where(ev_z, up, down)
        zo[x:x + 1, :] = jnp.where(ev_z, down, up)


def route(capacity, rows, devices, dest_h, seg_h, rec_h, send, slot_h, dest, seg, rec, slot_v, sems):
    panels = dest.shape[1]
    dest_in, seg_in, rec_in = fetch([dest_h, seg_h, rec_h], [dest, seg, rec], sems)
    dest_in.wait()
    seg_in.wait()
    d = dest[...]
    s = seg[...]
    hot = lax.broadcasted_iota(jnp.int32, (devices, panels), 0) == d
    hot_f = jnp.where(hot, 1.0, 0.0)
    before_me = lax.broadcasted_iota(jnp.int32, (panels, panels), 0) < lax.broadcasted_iota(
        jnp.int32, (panels, panels), 1
    )
    before = jnp.dot(
        hot_f.astype(BF16), jnp.where(before_me, 1.0, 0.0).astype(BF16), preferred_element_type=F32
    )
    slot = jnp.sum(before * hot_f, axis=0, keepdims=True).astype(jnp.int32)
    slot_v[...] = d * capacity + slot
    slot_out = pltpu.make_async_copy(slot_v, slot_h, sems.at[3])
    slot_out.start()
    place = d * rows + slot
    pick = lax.broadcasted_iota(jnp.int32, (devices * rows, panels), 0) == place
    rec_in.wait()
    records = jnp.dot(jnp.where(pick, 1.0, 0.0).astype(BF16), rec[...], preferred_element_type=F32)
    high = (s // DIGIT).astype(F32)
    low = (s % DIGIT).astype(F32)
    lane = lax.broadcasted_iota(jnp.int32, (LANES, panels), 0)
    at_high = jnp.where(lane == slot, 1.0, 0.0).astype(BF16)
    at_low = jnp.where(lane == slot + capacity, 1.0, 0.0).astype(BF16)
    contract = (((1,), (1,)), ((), ()))
    digits = lax.dot_general(
        (hot_f * high).astype(BF16), at_high, contract, preferred_element_type=F32
    ) + lax.dot_general((hot_f * low).astype(BF16), at_low, contract, preferred_element_type=F32)
    records = records.reshape(devices, rows, LANES)
    is_digit = lax.broadcasted_iota(jnp.int32, records.shape, 1) >= capacity
    send[...] = jnp.where(is_digit, digits[:, None, :], records).astype(BF16)
    slot_out.wait()


def parts_of(cells_x):
    step = max(1, cells_x // 4)
    return [(first, min(step, cells_x - first)) for first in range(0, cells_x, step)]


def fetch_field(source, target, sems, row):
    copies = []
    for n, (first, count) in enumerate(parts_of(target.shape[0])):
        planes = pl.ds(first, count)
        copies.append(pltpu.make_async_copy(source.at[planes], target.at[planes], sems.at[row, n]))
        copies[-1].start()
    return copies


def advect(
    alpha, vx, vz, p_h, xe_in, xo_in, ze_in, zo_in,
    out_h, xe, xo, ze, zo,
    out, p0, p1, pz0, pz1, sems, p_sems,
):
    cells_x, cells_z, beam = alpha.shape
    chunks = cells_z // SUB
    ev_x = even("slab")
    ev_z = even("depth")
    top = row_is((SUB, beam), 0)
    bottom = row_is((SUB, beam), SUB - 1)
    parts = parts_of(cells_x)
    p_ins = fetch(x_planes(p_h) + z_tiles(p_h), [p0, p1, pz0, pz1], p_sems)
    outs = [
        pltpu.make_async_copy(out.at[pl.ds(f, c)], out_h.at[pl.ds(f, c)], sems.at[n])
        for n, (f, c) in enumerate(parts)
    ]

    def at(k):
        return pl.ds(k * SUB, SUB)

    has_x, has_z = inner("slab"), inner("depth")

    def plane(x, first, last):
        zlo = has_z[0] * jnp.where(ev_z, zo_in[pl.ds(x, 1), :], ze_in[pl.ds(x, 1), :])
        zhi = has_z[1] * jnp.where(ev_z, ze_in[pl.ds(x, 1), :], zo_in[pl.ds(x, 1), :])
        above = None
        for k in reversed(range(chunks)):
            a = alpha[x, at(k), :]
            v = vx[x, at(k), :]
            if first:
                am = has_x[0] * jnp.where(ev_x, xo_in[at(k), :], xe_in[at(k), :]).astype(F32)
            else:
                am = alpha[x - 1, at(k), :]
            fx = v * jnp.where(v > 0, am, a)
            if last:
                q = has_x[1] * jnp.where(ev_x, xe_in[at(k), :], xo_in[at(k), :]).astype(F32)
                fxn = jnp.where(q > 0, q * a, q)
            else:
                vn = vx[x + 1, at(k), :]
                fxn = vn * jnp.where(vn > 0, a, alpha[x + 1, at(k), :])
            w = vz[x, at(k), :]
            if k == 0:
                edge = jnp.broadcast_to(zlo, a.shape)
            else:
                edge = pltpu.roll(alpha[x, at(k - 1), :], 1, 0)
            ad = jnp.where(top, edge, pltpu.roll(a, 1, 0))
            fz = w * jnp.where(w > 0, ad, a)
            up = pltpu.roll(fz, SUB - 1, 0)
            if above is None:
                q = jnp.broadcast_to(zhi, a.shape)
                fzn = jnp.where(bottom, jnp.where(q > 0, q * a, q), up)
            else:
                fzn = jnp.where(bottom, above, up)
            above = up
            new = a - COURANT * (fxn - fx + fzn - fz)
            out[x, at(k), :] = new
            if k == chunks - 1:
                z_up = new[SUB - 1:SUB, :] - 0.5
            if k == 0:
                z_down = new[0:1, :] - 0.5
        ze[0, pl.ds(x, 1), :] = jnp.where(ev_z, z_up, z_down)
        zo[0, pl.ds(x, 1), :] = jnp.where(ev_z, z_down, z_up)

    for n, (first, count) in enumerate(parts):
        begin = max(first - 1, 0)
        end = first + count - 1
        if begin == 0:
            plane(0, True, end == begin and cells_x == 1)
            begin = 1

        @pl.loop(begin, end)
        def _(x):
            plane(x, False, False)

        if n == len(parts) - 1:
            plane(cells_x - 1, False, True)
        if n > 0:
            outs[n - 1].start()
    outs[-1].start()

    for copy in p_ins:
        copy.wait()
    for k in range(chunks):
        for which, up, down in ((0, out[cells_x - 1, at(k), :] - 0.5, out[0, at(k), :] - 0.5), (1, p1[at(k), :], p0[at(k), :])):
            xe[which, at(k), :] = jnp.where(ev_x, up, down).astype(BF16)
            xo[which, at(k), :] = jnp.where(ev_x, down, up).astype(BF16)
    for x in range(cells_x):
        up = pz1[x, SUB - 1:SUB, :]
        down = pz0[x, 0:1, :]
        ze[1, x:x + 1, :] = jnp.where(ev_z, up, down)
        zo[1, x:x + 1, :] = jnp.where(ev_z, down, up)
    for copy in outs:
        copy.wait()


def coefficients(alpha_h, after, alpha, cx, cz, cy, inverse, sems):
    del after
    cells_x, cells_z, beam = alpha.shape
    chunks = cells_z // SUB
    top = row_is((SUB, beam), 0)
    bottom = row_is((SUB, beam), SUB - 1)
    lane = lax.broadcasted_iota(jnp.int32, (SUB, beam), 1)
    ins = fetch_field(alpha_h, alpha, sems, 0)
    cx[0] = jnp.zeros((cells_z, beam), F32)

    def at(k):
        return pl.ds(k * SUB, SUB)

    def plane(x):
        inside = jnp.where(x < cells_x - 1, 2.0, 0.0)
        nxt = jnp.minimum(x + 1, cells_x - 1)
        above = jnp.zeros((SUB, beam), F32)
        for k in reversed(range(chunks)):
            rho = 1.0 + 9.0 * alpha[x, at(k), :]
            rho_x = 1.0 + 9.0 * alpha[nxt, at(k), :]
            hx = inside / (rho + rho_x)
            cx[x + 1, at(k), :] = hx
            rolled = pltpu.roll(rho, 1, 0)
            if k == 0:
                hz = jnp.where(top, 0.0, 2.0 / (rho + rolled))
            else:
                below = pltpu.roll(1.0 + 9.0 * alpha[x, at(k - 1), :], 1, 0)
                hz = 2.0 / (rho + jnp.where(top, below, rolled))
            cz[x, at(k), :] = hz
            up = pltpu.roll(hz, SUB - 1, 0)
            hz_up = jnp.where(bottom, above, up)
            above = up
            hy_all = 2.0 / (rho + jnp.where(lane == 0, 0.0, pltpu.roll(rho, 1, 1)))
            hy = jnp.where(lane == 0, 0.0, hy_all)
            cy[x, at(k), :] = hy
            far = rho[:, beam - LANES:]
            edge = jnp.where(lane[:, beam - LANES:] == beam - 1, 2.0 / far, 0.0)
            hy_up = pltpu.roll(hy, beam - 1, 1)
            hy_up = jnp.concatenate(
                [hy_up[:, : beam - LANES], hy_up[:, beam - LANES:] + edge], axis=1
            )
            inverse[x, at(k), :] = 1.0 / (cx[x, at(k), :] + hx + hz + hz_up + hy_all + hy_up)

    parts = parts_of(cells_x)
    for n, (first, count) in enumerate(parts):
        ins[n].wait()
        end = cells_x if n == len(parts) - 1 else first + count - 1

        @pl.loop(max(first - 1, 0), end)
        def _(x):
            plane(x)


def close(
    p_in, inverse_in, alpha, xe_in, xo_in, ze_in, zo_in,
    p, inverse, gx, gz, xe, xo, ze, zo,
    wx,
):
    del p_in, inverse_in
    cells_x, cells_z, beam = alpha.shape
    chunks = cells_z // SUB
    ev_x, ev_z = even("slab"), even("depth")
    has = [inner("slab"), inner("depth")]

    def at(k):
        return pl.ds(k * SUB, SUB)

    for side, x in ((0, 0), (1, cells_x - 1)):
        for k in range(chunks):
            a, b = xe_in[:, at(k), :], xo_in[:, at(k), :]
            v = (jnp.where(ev_x, a, b) if side else jnp.where(ev_x, b, a)).astype(F32)
            halo = has[0][side] * (9.0 * v[0] + 5.5)
            c = 2.0 / (1.0 + 9.0 * alpha[x, at(k), :] + halo)
            w = 1.0 / inverse[x, at(k), :]
            open_c = has[0][side] * c
            p[x, at(k), :] = p[x, at(k), :] * w + open_c * v[1]
            gx[side, at(k), :] = open_c
            wx[side, at(k), :] = w + c

    def rows(x, plane):
        faces = []
        for side, k in ((0, 0), (1, chunks - 1)):
            here = row_is((SUB, beam), 0 if side == 0 else SUB - 1)
            a, b = ze_in[:, pl.ds(x, 1), :], zo_in[:, pl.ds(x, 1), :]
            v = jnp.where(ev_z, a, b) if side else jnp.where(ev_z, b, a)
            halo = jnp.broadcast_to(has[1][side] * (9.0 * v[0] + 5.5), (SUB, beam))
            c = jnp.where(here, 2.0 / (1.0 + 9.0 * alpha[x, at(k), :] + halo), 0.0)
            open_c = has[1][side] * c
            add = open_c * jnp.broadcast_to(v[1], (SUB, beam))
            if plane is None:
                w = 1.0 / inverse[x, at(k), :]
                total = p[x, at(k), :] * w + add
                inv = 1.0 / (w + c)
                inverse[x, at(k), :] = inv
                new = total * inv
                p[x, at(k), :] = new
            else:
                w = wx[plane, at(k), :] + c
                wx[plane, at(k), :] = w
                inv = 1.0 / w
                total = p[x, at(k), :] + add
                p[x, at(k), :] = total
                new = total * inv
            g = inv * open_c
            r = slice(0, 1) if side == 0 else slice(SUB - 1, SUB)
            gz[side, pl.ds(x, 1), :] = g[r, :]
            faces.append(new[r, :])
        ze[pl.ds(x, 1), :] = jnp.where(ev_z, faces[1], faces[0])
        zo[pl.ds(x, 1), :] = jnp.where(ev_z, faces[0], faces[1])

    rows(0, 0)
    rows(cells_x - 1, 1)

    @pl.loop(1, cells_x - 1)
    def _(x):
        rows(x, None)

    for k in range(chunks):
        new = []
        for side, x in ((0, 0), (1, cells_x - 1)):
            inv = 1.0 / wx[side, at(k), :]
            inverse[x, at(k), :] = inv
            gx[side, at(k), :] = gx[side, at(k), :] * inv
            new.append(p[x, at(k), :] * inv)
            p[x, at(k), :] = new[side]
        xe[at(k), :] = jnp.where(ev_x, new[1], new[0]).astype(BF16)
        xo[at(k), :] = jnp.where(ev_x, new[0], new[1]).astype(BF16)


def by_lanes(ref):
    cells_x, cells_z, beam = ref.shape
    blocks = beam // LANES
    for b in range(blocks):
        yield b, pl.ds(b * LANES, LANES)


def scatter(capacity, got, div_h, rhs, row_out, rec32, row_v, row_s, hull, div, sems, sem):
    devices, rows, _ = got.shape
    cells_x, cells_z, beam = rhs.shape
    blocks = beam // LANES
    ins = fetch_field(div_h, div, sems, 0)
    digits = got[:, rows - 1, :].astype(F32)
    seg = (digits * float(DIGIT) + pltpu.roll(digits, LANES - capacity, 1)).astype(jnp.int32)
    across = seg // blocks
    row = ((across // cells_z) * blocks + seg % blocks) * cells_z + across % cells_z
    row_v[...] = row
    row_out[...] = row
    copy = pltpu.make_async_copy(row_v, row_s, sem)
    copy.start()
    rec32[...] = got[...].astype(F32).reshape(devices * rows, LANES)
    hull[...] = jnp.zeros_like(hull)
    copy.wait()

    @pl.loop(0, devices)
    def _(d):
        for s in range(capacity):
            n = row_s[d, s]
            hull[pl.ds(n, 1), :] += rec32[pl.ds(d * rows + s, 1), :]

    for copy in ins:
        copy.wait()

    @pl.loop(0, cells_x)
    def _(x):
        for b, lanes in by_lanes(rhs):
            first = pl.multiple_of((x * blocks + b) * cells_z, SUB)
            rhs[x, :, lanes] = div[x, :, lanes] + hull[pl.ds(first, cells_z), :]


def sweep(p, cx, cz, cy, inverse, rhs, out):
    cells_x, cells_z, beam = p.shape
    chunks = cells_z // SUB
    top = row_is((SUB, beam), 0)
    bottom = row_is((SUB, beam), SUB - 1)

    def at(k):
        return pl.ds(k * SUB, SUB)

    @pl.loop(0, cells_x)
    def _(x):
        prv = jnp.maximum(x - 1, 0)
        nxt = jnp.minimum(x + 1, cells_x - 1)
        above = jnp.zeros((SUB, beam), F32)
        rolled = pltpu.roll(p[x, at(chunks - 1), :], 1, 0)
        for k in reversed(range(chunks)):
            here = p[x, at(k), :]
            hz = cz[x, at(k), :]
            hy = cy[x, at(k), :]
            total = cx[x, at(k), :] * p[prv, at(k), :] + cx[x + 1, at(k), :] * p[nxt, at(k), :]
            if k > 0:
                below = pltpu.roll(p[x, at(k - 1), :], 1, 0)
                down = jnp.where(top, below, rolled)
                rolled = below
            else:
                down = rolled
            up = pltpu.roll(hz * here, SUB - 1, 0)
            total = total + (hz * down + jnp.where(bottom, above, up))
            above = up
            total = total + (hy * pltpu.roll(here, 1, 1) + pltpu.roll(hy * here, beam - 1, 1))
            out[x, at(k), :] = (total - rhs[x, at(k), :]) * inverse[x, at(k), :]


def add_borders(p_in, xe_in, xo_in, ze_in, zo_in, gx, gz, p, send=None):
    del p_in
    cells_x, cells_z, beam = p.shape
    chunks = cells_z // SUB
    ev_x, ev_z = even("slab"), even("depth")

    def at(k):
        return pl.ds(k * SUB, SUB)

    for side, x in ((0, 0), (1, cells_x - 1)):
        for k in range(chunks):
            a, b = xe_in[at(k), :], xo_in[at(k), :]
            v = jnp.where(ev_x, a, b) if side else jnp.where(ev_x, b, a)
            p[x, at(k), :] = p[x, at(k), :] + gx[side, at(k), :] * v.astype(F32)

    @pl.loop(0, cells_x)
    def _(x):
        faces = []
        for side, k in ((0, 0), (1, chunks - 1)):
            here = row_is((SUB, beam), 0 if side == 0 else SUB - 1)
            a, b = ze_in[pl.ds(x, 1), :], zo_in[pl.ds(x, 1), :]
            v = jnp.where(ev_z, a, b) if side else jnp.where(ev_z, b, a)
            add = jnp.broadcast_to(gz[side, pl.ds(x, 1), :] * v, (SUB, beam))
            new = p[x, at(k), :] + jnp.where(here, add, 0.0)
            p[x, at(k), :] = new
            faces.append(new[0:1, :] if side == 0 else new[SUB - 1:SUB, :])
        if send is not None:
            send[2][pl.ds(x, 1), :] = jnp.where(ev_z, faces[1], faces[0])
            send[3][pl.ds(x, 1), :] = jnp.where(ev_z, faces[0], faces[1])

    if send is not None:
        for k in range(chunks):
            lo, hi = p[0, at(k), :], p[cells_x - 1, at(k), :]
            send[0][at(k), :] = jnp.where(ev_x, hi, lo).astype(BF16)
            send[1][at(k), :] = jnp.where(ev_x, lo, hi).astype(BF16)


def fix_and_send(p_in, xe_in, xo_in, ze_in, zo_in, gx, gz, p, xe, xo, ze, zo):
    add_borders(p_in, xe_in, xo_in, ze_in, zo_in, gx, gz, p, (xe, xo, ze, zo))


def fix_and_gather(
    capacity, p_in, xe_in, xo_in, ze_in, zo_in, gx, gz, row, p_h, back, p, split, rows32, sems
):
    cells_x, cells_z, beam = p.shape
    p[...] = p_in[...]
    add_borders(p_in, xe_in, xo_in, ze_in, zo_in, gx, gz, p)
    blocks = beam // LANES
    devices = back.shape[0]
    out = pltpu.make_async_copy(p, p_h, sems)
    out.start()

    @pl.loop(0, cells_x)
    def _(x):
        for b, lanes in by_lanes(p):
            first = pl.multiple_of((x * blocks + b) * cells_z, SUB)
            split[pl.ds(first, cells_z), :] = p[x, :, lanes]

    @pl.loop(0, devices)
    def _(d):
        for s in range(capacity):
            rows32[pl.ds(d * capacity + s, 1), :] = split[pl.ds(row[d, s], 1), :]

    back[...] = rows32[...].astype(BF16).reshape(back.shape)
    out.wait()


def unroute(back, slot, out):
    rows = back.shape[0] * back.shape[1]
    panels = out.shape[0]
    pick = lax.broadcasted_iota(jnp.int32, (rows, panels), 0) == slot[...]
    out[...] = lax.dot_general(
        jnp.where(pick, 1.0, 0.0).astype(BF16),
        back[...].reshape(rows, LANES),
        (((0,), (0,)), ((), ())),
        preferred_element_type=F32,
    ).astype(BF16)


def body(alpha, vel_x, vel_z, divergence, press_guess, panel_records, panel_dest, panel_segment):
    devices = lax.axis_size("slab") * lax.axis_size("depth")
    panels = panel_records.shape[0]
    capacity = 2 * panels // devices
    cells_x, cells_z, beam = alpha.shape
    field = shape(alpha.shape)
    rows = -(-(capacity + 1) // SUB) * SUB
    axes = ("slab", "depth")

    xs, zs = (cells_z, beam), (cells_x, beam)
    tile = (cells_x, SUB, beam)
    faces = [shape(xs, BF16)] * 2 + [shape(zs)] * 2
    two_faces = [shape((2,) + xs, BF16)] * 2 + [shape((2,) + zs)] * 2
    parts = len(parts_of(cells_x))
    lines = (cells_x * cells_z * beam // LANES, LANES)

    def near(dims, dtype=F32):
        return pltpu.VMEM(tuple(dims), dtype)

    def swaps(xe, xo, ze, zo):
        return swap(xe, "slab", 0), swap(xo, "slab", 1), swap(ze, "depth", 0), swap(zo, "depth", 1)

    send, slot = call(
        functools.partial(route, capacity, rows, devices),
        [shape((devices, rows, LANES), BF16), shape((1, panels), jnp.int32)],
        panel_dest.reshape(1, panels), panel_segment.reshape(1, panels), panel_records,
        far_in=(0, 1, 2), free_out=(0,), far_out=(1,),
        scratch=[
            near((1, panels), jnp.int32),
            near((1, panels), jnp.int32),
            near((panels, LANES), BF16),
            near((1, panels), jnp.int32),
            DMA((4,)),
        ],
        name="route",
    )
    got = lax.all_to_all(send, axes, split_axis=0, concat_axis=0, tiled=True)

    packed = call(
        pack_first, faces, alpha, vel_x, vel_z,
        far_in=(0, 1, 2),
        scratch=[near(xs), near(xs), near(tile), near(tile), near(xs), near(tile), DMA((6,))],
        name="pack_first",
    )
    alpha_next, *packed = call(
        advect, [field] + two_faces, alpha, vel_x, vel_z, press_guess, *swaps(*packed),
        far_in=(3,), far_out=(0,),
        scratch=[near(alpha.shape), near(xs), near(xs), near(tile), near(tile), DMA((parts,)), DMA((4,))],
        name="advect",
    )
    halo = swaps(*packed)
    near_alpha, cx, cz, cy, inverse = call(
        coefficients,
        [field, shape((cells_x + 1,) + xs), field, field, field],
        alpha_next, got,
        far_in=(0,),
        in_specs={1: pl.BlockSpec(memory_space=pl.ANY)},
        scratch=[DMA((1, parts))],
        name="coefficients",
    )
    rhs, row = call(
        functools.partial(scatter, capacity),
        [field, shape((devices, LANES), jnp.int32)],
        got, divergence,
        far_in=(1,),
        scratch=[
            near((devices * rows, LANES)),
            near((devices, LANES), jnp.int32),
            pltpu.SMEM((devices, LANES), jnp.int32),
            near(lines),
            near(alpha.shape),
            DMA((1, parts)),
            DMA,
        ],
        name="scatter",
    )
    (pressure,) = call(sweep, [field], press_guess, cx, cz, cy, inverse, rhs, name="sweep")
    pressure, inverse, gx, gz, *packed = call(
        close,
        [field, field, shape((2,) + xs), shape((2,) + zs)] + faces,
        pressure, inverse, near_alpha, *halo,
        aliases={0: 0, 1: 1},
        scratch=[near((2,) + xs)],
        name="close",
    )
    halo = swaps(*packed)
    (pressure,) = call(sweep, [field], pressure, cx, cz, cy, inverse, rhs, name="sweep")
    pressure, *packed = call(
        fix_and_send, [field] + faces, pressure, *halo, gx, gz, aliases={0: 0}, name="fix"
    )
    halo = swaps(*packed)
    (pressure,) = call(sweep, [field], pressure, cx, cz, cy, inverse, rhs, name="sweep")
    pressure, back = call(
        functools.partial(fix_and_gather, capacity),
        [field, shape((devices, capacity, LANES), BF16)],
        pressure, *halo, gx, gz, row,
        far_out=(0,),
        in_specs={7: pl.BlockSpec(memory_space=pltpu.SMEM)},
        scratch=[near(alpha.shape), near(lines), near((devices * capacity, LANES)), DMA],
        name="gather",
    )
    returned = lax.all_to_all(back, axes, split_axis=0, concat_axis=0, tiled=True)
    panel_pressure = pl.pallas_call(
        unroute,
        out_shape=shape((panels, LANES), BF16),
        in_specs=[WHOLE] * 2,
        out_specs=WHOLE,
        name="unroute",
    )(returned, slot)
    return (pressure, alpha_next, panel_pressure)


def solution(mesh):
    in_specs = (
        P("slab", "depth", None),
        P("slab", "depth", None),
        P("slab", "depth", None),
        P("slab", "depth", None),
        P("slab", "depth", None),
        P(("slab", "depth"), None),
        P(("slab", "depth"), None),
        P(("slab", "depth"), None),
    )
    out_specs = (P("slab", "depth", None), P("slab", "depth", None), P(("slab", "depth"), None))
    return jax.shard_map(body, mesh=mesh, in_specs=in_specs, out_specs=out_specs, check_vma=False)
```

```python
import functools

import jax
import jax.numpy as jnp
from jax import lax
from jax.experimental import pallas as pl
from jax.experimental.pallas import tpu as pltpu
from jax.sharding import PartitionSpec as P


COURANT = 0.2
LANES = 128
SUB = 8
DIGIT = 256
MIB = 1 << 20
F32 = jnp.float32
BF16 = jnp.bfloat16

WHOLE = pl.BlockSpec(memory_space=pltpu.VMEM)
FAR = pl.BlockSpec(memory_space=pltpu.HBM)
DMA = pltpu.SemaphoreType.DMA


def call(kernel, outs, *args, aliases=None, far_in=(), far_out=(), free_out=(), in_specs=None, scratch=(), limit=12 * MIB):
    specs = [FAR if n in far_in else WHOLE for n in range(len(args))]
    for n, spec in (in_specs or {}).items():
        specs[n] = spec
    shapes = [o if n in far_out or n in free_out else pltpu.VMEM(o.shape, o.dtype) for n, o in enumerate(outs)]
    return pl.pallas_call(
        kernel,
        out_shape=shapes,
        in_specs=specs,
        out_specs=[FAR if n in far_out else WHOLE for n in range(len(outs))],
        scratch_shapes=list(scratch),
        input_output_aliases=aliases or {},
        compiler_params=pltpu.CompilerParams(vmem_limit_bytes=limit),
    )(*(pltpu.with_memory_space_constraint(a, pltpu.HBM) if n in far_in else a for n, a in enumerate(args)))


def shape(dims, dtype=F32):
    return jax.ShapeDtypeStruct(tuple(dims), dtype)


def even(axis):
    return lax.rem(lax.axis_index(axis), 2) == 0


def swap(block, axis, odd):
    slabs, depths = lax.axis_size("slab"), lax.axis_size("depth")
    pairs = []
    for i in range(slabs):
        for j in range(depths):
            own, count, other = (i, slabs, depths) if axis == "slab" else (j, depths, slabs)
            partner = own + 1 if own % 2 == odd else own - 1
            target = (partner, j) if axis == "slab" else (i, partner)
            if not 0 <= partner < count:
                if other % 2:
                    continue
                target = (i, j ^ 1) if axis == "slab" else (i ^ 1, j)
            pairs.append((i * depths + j, target[0] * depths + target[1]))
    return lax.ppermute(block, ("slab", "depth"), pairs)


def inner(axis):
    i = lax.axis_index(axis)
    return [jnp.where(i > 0, 1.0, 0.0), jnp.where(i < lax.axis_size(axis) - 1, 1.0, 0.0)]


def unrolled(begin, end, most=4):
    count = end - begin
    return pl.loop(begin, end, unroll=next(n for n in range(most, 0, -1) if count % n == 0))


def row_is(rows, index):
    return lax.broadcasted_iota(jnp.int32, rows, 0) == index


def z_tiles(ref):
    last = ref.shape[1] // SUB - 1
    return [ref.at[:, pl.ds(0, SUB), :], ref.at[:, pl.ds(last * SUB, SUB), :]]


def x_planes(ref):
    return [ref.at[0], ref.at[ref.shape[0] - 1]]


def fetch(sources, targets, sems):
    copies = []
    for n, (source, target) in enumerate(zip(sources, targets)):
        copies.append(pltpu.make_async_copy(source, target, sems.at[n]))
        copies[-1].start()
    return copies


def pack_first(a0, a1, az0, az1, vx0, vz0, xe, xo, ze, zo):
    ev_x = even("slab")
    ev_z = even("depth")

    def fold(v, a):
        return jnp.where(v > 0, v, v * a)

    for k in range(a0.shape[0] // SUB):
        at = pl.ds(k * SUB, SUB)
        up = a1[at, :]
        down = fold(vx0[at, :], a0[at, :])
        xe[at, :] = jnp.where(ev_x, up, down).astype(BF16)
        xo[at, :] = jnp.where(ev_x, down, up).astype(BF16)
    for x in range(az0.shape[0]):
        up = az1[x, SUB - 1:SUB, :]
        down = fold(vz0[x, 0:1, :], az0[x, 0:1, :])
        ze[x:x + 1, :] = jnp.where(ev_z, up, down)
        zo[x:x + 1, :] = jnp.where(ev_z, down, up)


def enter(
    capacity, rows, devices,
    alpha, vx, vz, dest_h, seg_h, rec_h,
    xe, xo, ze, zo, send_h, slot_h,
    a0, a1, az0, az1, vx0, vz0, dest, seg, rec, slot_v, send, sems,
):
    sources = x_planes(alpha) + z_tiles(alpha) + x_planes(vx)[:1] + z_tiles(vz)[:1]
    borders = [a0, a1, az0, az1, vx0, vz0]
    copies = fetch([dest_h, seg_h, rec_h] + sources, [dest, seg, rec] + borders, sems)
    panels = dest.shape[1]
    copies[0].wait()
    copies[1].wait()
    d = dest[...]
    s = seg[...]
    hot = lax.broadcasted_iota(jnp.int32, (devices, panels), 0) == d
    hot_f = jnp.where(hot, 1.0, 0.0)
    before_me = lax.broadcasted_iota(jnp.int32, (panels, panels), 0) < lax.broadcasted_iota(
        jnp.int32, (panels, panels), 1
    )
    before = jnp.dot(
        hot_f.astype(BF16), jnp.where(before_me, 1.0, 0.0).astype(BF16), preferred_element_type=F32
    )
    slot = jnp.sum(before * hot_f, axis=0, keepdims=True).astype(jnp.int32)
    slot_v[...] = d * capacity + slot
    slot_out = pltpu.make_async_copy(slot_v, slot_h, sems.at[9])
    slot_out.start()
    place = d * rows + slot
    pick = lax.broadcasted_iota(jnp.int32, (devices * rows, panels), 0) == place
    copies[2].wait()
    records = jnp.dot(jnp.where(pick, 1.0, 0.0).astype(BF16), rec[...], preferred_element_type=F32)
    high = (s // DIGIT + 1).astype(F32)
    low = (s % DIGIT).astype(F32)
    lane = lax.broadcasted_iota(jnp.int32, (LANES, panels), 0)
    at_high = jnp.where(lane == slot, 1.0, 0.0).astype(BF16)
    at_low = jnp.where(lane == slot + capacity, 1.0, 0.0).astype(BF16)
    contract = (((1,), (1,)), ((), ()))
    digits = lax.dot_general(
        (hot_f * high).astype(BF16), at_high, contract, preferred_element_type=F32
    ) + lax.dot_general((hot_f * low).astype(BF16), at_low, contract, preferred_element_type=F32)
    records = records.reshape(devices, rows, LANES)
    is_digit = lax.broadcasted_iota(jnp.int32, records.shape, 1) >= capacity
    send[...] = jnp.where(is_digit, digits[:, None, :], records).astype(BF16)
    send_out = pltpu.make_async_copy(send, send_h, sems.at[10])
    send_out.start()
    for copy in copies[3:]:
        copy.wait()
    pack_first(*borders, xe, xo, ze, zo)
    slot_out.wait()
    send_out.wait()


def parts_of(cells_x):
    step = max(1, cells_x // 8)
    return [(first, min(step, cells_x - first)) for first in range(0, cells_x, step)]


def fetch_fields(fields, sems):
    copies = [[] for _ in fields]
    for n, (first, count) in enumerate(parts_of(fields[0][1].shape[0])):
        planes = pl.ds(first, count)
        for row, (source, target) in enumerate(fields):
            copy = pltpu.make_async_copy(source.at[planes], target.at[planes], sems.at[row, n])
            copy.start()
            copies[row].append(copy)
    return copies


def advect(
    alpha_h, vx_h, vz_h, p_h, xe_in, xo_in, ze_in, zo_in,
    out_h, xe, xo, ze, zo,
    alpha, vx, vz, out, p0, p1, pz0, pz1, sems, p_sems,
):
    cells_x, cells_z, beam = alpha.shape
    chunks = cells_z // SUB
    ev_x = even("slab")
    ev_z = even("depth")
    top = row_is((SUB, beam), 0)
    bottom = row_is((SUB, beam), SUB - 1)
    parts = parts_of(cells_x)
    fields = ((alpha_h, alpha), (vx_h, vx), (vz_h, vz))
    ins = fetch_fields(fields, sems)
    p_ins = fetch(x_planes(p_h) + z_tiles(p_h), [p0, p1, pz0, pz1], p_sems)
    outs = [
        pltpu.make_async_copy(out.at[pl.ds(f, c)], out_h.at[pl.ds(f, c)], sems.at[len(fields), n])
        for n, (f, c) in enumerate(parts)
    ]

    def at(k):
        return pl.ds(k * SUB, SUB)

    has_x, has_z = inner("slab"), inner("depth")

    def plane(x, first, last):
        zlo = has_z[0] * jnp.where(ev_z, zo_in[pl.ds(x, 1), :], ze_in[pl.ds(x, 1), :])
        zhi = has_z[1] * jnp.where(ev_z, ze_in[pl.ds(x, 1), :], zo_in[pl.ds(x, 1), :])
        above = None
        for k in reversed(range(chunks)):
            a = alpha[x, at(k), :]
            v = vx[x, at(k), :]
            if first:
                am = has_x[0] * jnp.where(ev_x, xo_in[at(k), :], xe_in[at(k), :]).astype(F32)
            else:
                am = alpha[x - 1, at(k), :]
            fx = v * jnp.where(v > 0, am, a)
            if last:
                q = has_x[1] * jnp.where(ev_x, xe_in[at(k), :], xo_in[at(k), :]).astype(F32)
                fxn = jnp.where(q > 0, q * a, q)
            else:
                vn = vx[x + 1, at(k), :]
                fxn = vn * jnp.where(vn > 0, a, alpha[x + 1, at(k), :])
            w = vz[x, at(k), :]
            if k == 0:
                edge = jnp.broadcast_to(zlo, a.shape)
            else:
                edge = pltpu.roll(alpha[x, at(k - 1), :], 1, 0)
            ad = jnp.where(top, edge, pltpu.roll(a, 1, 0))
            fz = w * jnp.where(w > 0, ad, a)
            up = pltpu.roll(fz, SUB - 1, 0)
            if above is None:
                q = jnp.broadcast_to(zhi, a.shape)
                fzn = jnp.where(bottom, jnp.where(q > 0, q * a, q), up)
            else:
                fzn = jnp.where(bottom, above, up)
            above = up
            new = a - COURANT * (fxn - fx + fzn - fz)
            out[x, at(k), :] = new
            if k == chunks - 1:
                z_up = new[SUB - 1:SUB, :] - 0.5
            if k == 0:
                z_down = new[0:1, :] - 0.5
        ze[0, pl.ds(x, 1), :] = jnp.where(ev_z, z_up, z_down)
        zo[0, pl.ds(x, 1), :] = jnp.where(ev_z, z_down, z_up)

    for n, (first, count) in enumerate(parts):
        for copies in ins:
            copies[n].wait()
        begin = max(first - 1, 0)
        end = first + count - 1
        if begin == 0:
            plane(0, True, end == begin and cells_x == 1)
            begin = 1

        @pl.loop(begin, end)
        def _(x):
            plane(x, False, False)

        if n == len(parts) - 1:
            plane(cells_x - 1, False, True)
        if n > 0:
            outs[n - 1].start()
    outs[-1].start()

    for copy in p_ins:
        copy.wait()
    for k in range(chunks):
        for which, up, down in ((0, out[cells_x - 1, at(k), :] - 0.5, out[0, at(k), :] - 0.5), (1, p1[at(k), :], p0[at(k), :])):
            xe[which, at(k), :] = jnp.where(ev_x, up, down).astype(BF16)
            xo[which, at(k), :] = jnp.where(ev_x, down, up).astype(BF16)
    for x in range(cells_x):
        up = pz1[x, SUB - 1:SUB, :]
        down = pz0[x, 0:1, :]
        ze[1, x:x + 1, :] = jnp.where(ev_z, up, down)
        zo[1, x:x + 1, :] = jnp.where(ev_z, down, up)
    for copy in outs:
        copy.wait()


def coefficients(half, cx, cz, cy, inverse, arrived):
    cells_x, cells_z, beam = half.shape
    chunks = cells_z // SUB
    top = row_is((SUB, beam), 0)
    bottom = row_is((SUB, beam), SUB - 1)
    lane = lax.broadcasted_iota(jnp.int32, (SUB, beam), 1)
    end_lane = lane[:, beam - LANES:] == beam - 1
    none = jnp.zeros((cells_z, beam), F32)
    cx[0] = none
    cx[cells_x] = none

    def at(k):
        return pl.ds(k * SUB, SUB)

    def plane(x, last):
        above = jnp.zeros((SUB, beam), F32)
        for k in reversed(range(chunks)):
            r = half[x, at(k), :]
            total = cx[x, at(k), :]
            if not last:
                hx = 1.0 / (r + half[x + 1, at(k), :])
                cx[x + 1, at(k), :] = hx
                total = total + hx
            rolled = pltpu.roll(r, 1, 0)
            if k == 0:
                hz = jnp.where(top, 0.0, 1.0 / (r + rolled))
            else:
                below = pltpu.roll(half[x, at(k - 1), :], 1, 0)
                hz = 1.0 / (r + jnp.where(top, below, rolled))
            cz[x, at(k), :] = hz
            up = pltpu.roll(hz, SUB - 1, 0)
            total = total + (hz + jnp.where(bottom, above, up))
            above = up
            hy_all = 1.0 / (r + jnp.where(lane == 0, 0.0, pltpu.roll(r, 1, 1)))
            hy = jnp.where(lane == 0, 0.0, hy_all)
            cy[x, at(k), :] = hy
            edge = jnp.where(end_lane, 1.0 / r[:, beam - LANES:], 0.0)
            hy_up = pltpu.roll(hy, beam - 1, 1)
            hy_up = jnp.concatenate(
                [hy_up[:, : beam - LANES], hy_up[:, beam - LANES:] + edge], axis=1
            )
            inverse[x, at(k), :] = 1.0 / (total + (hy_all + hy_up))

    begin = 0
    for stop in arrived():
        @unrolled(begin, stop - 1, 3)
        def _(x):
            plane(x, False)

        begin = stop - 1
    plane(cells_x - 1, True)


def close(
    p_in, inverse_in, half, xe_in, xo_in, ze_in, zo_in,
    p, inverse, gx, gz, xe, xo, ze, zo,
    wx,
):
    del p_in, inverse_in
    cells_x, cells_z, beam = half.shape
    chunks = cells_z // SUB
    ev_x, ev_z = even("slab"), even("depth")
    has = [inner("slab"), inner("depth")]

    def at(k):
        return pl.ds(k * SUB, SUB)

    for side, x in ((0, 0), (1, cells_x - 1)):
        for k in range(chunks):
            a, b = xe_in[:, at(k), :], xo_in[:, at(k), :]
            v = (jnp.where(ev_x, a, b) if side else jnp.where(ev_x, b, a)).astype(F32)
            halo = has[0][side] * (4.5 * v[0] + 2.75)
            c = 1.0 / (half[x, at(k), :] + halo)
            w = 1.0 / inverse[x, at(k), :]
            open_c = has[0][side] * c
            p[x, at(k), :] = p[x, at(k), :] * w + open_c * v[1]
            gx[side, at(k), :] = open_c
            wx[side, at(k), :] = w + c

    def rows(x, plane):
        faces = []
        for side, k in ((0, 0), (1, chunks - 1)):
            here = row_is((SUB, beam), 0 if side == 0 else SUB - 1)
            a, b = ze_in[:, pl.ds(x, 1), :], zo_in[:, pl.ds(x, 1), :]
            v = jnp.where(ev_z, a, b) if side else jnp.where(ev_z, b, a)
            halo = jnp.broadcast_to(has[1][side] * (4.5 * v[0] + 2.75), (SUB, beam))
            c = jnp.where(here, 1.0 / (half[x, at(k), :] + halo), 0.0)
            open_c = has[1][side] * c
            add = open_c * jnp.broadcast_to(v[1], (SUB, beam))
            if plane is None:
                w = 1.0 / inverse[x, at(k), :]
                total = p[x, at(k), :] * w + add
                inv = 1.0 / (w + c)
                inverse[x, at(k), :] = inv
                new = total * inv
                p[x, at(k), :] = new
            else:
                w = wx[plane, at(k), :] + c
                wx[plane, at(k), :] = w
                inv = 1.0 / w
                total = p[x, at(k), :] + add
                p[x, at(k), :] = total
                new = total * inv
            g = inv * open_c
            r = slice(0, 1) if side == 0 else slice(SUB - 1, SUB)
            gz[side, pl.ds(x, 1), :] = g[r, :]
            faces.append(new[r, :])
        ze[pl.ds(x, 1), :] = jnp.where(ev_z, faces[1], faces[0])
        zo[pl.ds(x, 1), :] = jnp.where(ev_z, faces[0], faces[1])

    rows(0, 0)
    rows(cells_x - 1, 1)

    @pl.loop(1, cells_x - 1)
    def _(x):
        rows(x, None)

    for k in range(chunks):
        new = []
        for side, x in ((0, 0), (1, cells_x - 1)):
            inv = 1.0 / wx[side, at(k), :]
            inverse[x, at(k), :] = inv
            gx[side, at(k), :] = gx[side, at(k), :] * inv
            new.append(p[x, at(k), :] * inv)
            p[x, at(k), :] = new[side]
        xe[at(k), :] = jnp.where(ev_x, new[1], new[0]).astype(BF16)
        xo[at(k), :] = jnp.where(ev_x, new[0], new[1]).astype(BF16)


def by_lanes(ref):
    _, _, beam = ref.shape
    blocks = beam // LANES
    for b in range(blocks):
        yield b, pl.ds(b * LANES, LANES)


def middle(
    capacity, got, alpha_h, div_h, p_h,
    half, cx, cz, cy, inverse, rhs, p, row_out,
    rec32, row_v, row_s, hull, div, p0, sems, sem,
):
    devices, rows, _ = got.shape
    cells_x, cells_z, beam = rhs.shape
    blocks = beam // LANES
    digits = got[:, rows - 1, :].astype(F32)
    seg = (digits * float(DIGIT) + pltpu.roll(digits, LANES - capacity, 1)).astype(jnp.int32) - DIGIT
    across = seg // blocks
    row = ((across // cells_z) * blocks + seg % blocks) * cells_z + across % cells_z
    slots = lax.broadcasted_iota(jnp.int32, seg.shape, 0) * capacity
    slots = slots + lax.broadcasted_iota(jnp.int32, seg.shape, 1)
    row = jnp.where(seg < 0, slots % hull.shape[0], row)
    row_v[...] = row
    row_out[...] = row
    copy = pltpu.make_async_copy(row_v, row_s, sem)
    copy.start()
    cut = max(1, cells_x // 4)
    parts = [(0, cut), (cut, cells_x)]
    alpha_in = fetch(
        [alpha_h.at[pl.ds(i, j - i)] for i, j in parts], [half.at[pl.ds(i, j - i)] for i, j in parts], sems
    )
    rest = [
        pltpu.make_async_copy(h, v, sems.at[2 + n]) for n, (h, v) in enumerate(((div_h, div), (p_h, p0)))
    ]
    for other in rest:
        other.start()
    rec32[...] = got[...].astype(F32).reshape(devices * rows, LANES)
    hull[...] = jnp.zeros_like(hull)

    def arrived():
        for (i, j), part in zip(parts, alpha_in):
            part.wait()

            @unrolled(i, j)
            def _(x):
                half[x] = 0.5 + 4.5 * half[x]

            yield j

    coefficients(half, cx, cz, cy, inverse, arrived)
    copy.wait()

    @pl.loop(0, devices)
    def _(d):
        for s in range(capacity):
            n = row_s[d, s]
            hull[pl.ds(n, 1), :] += rec32[pl.ds(d * rows + s, 1), :]

    for other in rest:
        other.wait()

    def source(x, at):
        parts = []
        for b, lanes in by_lanes(rhs):
            first = pl.multiple_of((x * blocks + b) * cells_z + at.start, SUB)
            parts.append(div[x, at, lanes] + hull[pl.ds(first, SUB), :])
        value = jnp.concatenate(parts, axis=1)
        rhs[x, at, :] = value
        return value

    sweep(p0, cx, cz, cy, inverse, source, p)


def sweep(p, cx, cz, cy, inverse, source, out, start=0, stop=None):
    cells_x, cells_z, beam = p.shape
    chunks = cells_z // SUB
    top = row_is((SUB, beam), 0)
    bottom = row_is((SUB, beam), SUB - 1)

    def at(k):
        return pl.ds(k * SUB, SUB)

    @unrolled(start, cells_x if stop is None else stop)
    def _(x):
        prv = jnp.maximum(x - 1, 0)
        nxt = jnp.minimum(x + 1, cells_x - 1)
        above = jnp.zeros((SUB, beam), F32)
        rolled = pltpu.roll(p[x, at(chunks - 1), :], 1, 0)
        for k in reversed(range(chunks)):
            here = p[x, at(k), :]
            hz = cz[x, at(k), :]
            hy = cy[x, at(k), :]
            total = cx[x, at(k), :] * p[prv, at(k), :] + cx[x + 1, at(k), :] * p[nxt, at(k), :]
            if k > 0:
                below = pltpu.roll(p[x, at(k - 1), :], 1, 0)
                down = jnp.where(top, below, rolled)
                rolled = below
            else:
                down = rolled
            up = pltpu.roll(hz * here, SUB - 1, 0)
            total = total + (hz * down + jnp.where(bottom, above, up))
            above = up
            total = total + (hy * pltpu.roll(here, 1, 1) + pltpu.roll(hy * here, beam - 1, 1))
            out[x, at(k), :] = (total - source(x, at(k))) * inverse[x, at(k), :]


def next_sweep(p, cx, cz, cy, inverse, rhs, out):
    sweep(p, cx, cz, cy, inverse, lambda x, at: rhs[x, at, :], out)


def add_borders(p_in, xe_in, xo_in, ze_in, zo_in, gx, gz, p, send=None):
    del p_in
    cells_x, cells_z, beam = p.shape
    chunks = cells_z // SUB
    ev_x, ev_z = even("slab"), even("depth")

    def at(k):
        return pl.ds(k * SUB, SUB)

    for side, x in ((0, 0), (1, cells_x - 1)):
        for k in range(chunks):
            a, b = xe_in[at(k), :], xo_in[at(k), :]
            v = jnp.where(ev_x, a, b) if side else jnp.where(ev_x, b, a)
            p[x, at(k), :] = p[x, at(k), :] + gx[side, at(k), :] * v.astype(F32)

    @pl.loop(0, cells_x)
    def _(x):
        faces = []
        for side, k in ((0, 0), (1, chunks - 1)):
            here = row_is((SUB, beam), 0 if side == 0 else SUB - 1)
            a, b = ze_in[pl.ds(x, 1), :], zo_in[pl.ds(x, 1), :]
            v = jnp.where(ev_z, a, b) if side else jnp.where(ev_z, b, a)
            add = jnp.broadcast_to(gz[side, pl.ds(x, 1), :] * v, (SUB, beam))
            new = p[x, at(k), :] + jnp.where(here, add, 0.0)
            p[x, at(k), :] = new
            faces.append(new[0:1, :] if side == 0 else new[SUB - 1:SUB, :])
        if send is not None:
            send[2][pl.ds(x, 1), :] = jnp.where(ev_z, faces[1], faces[0])
            send[3][pl.ds(x, 1), :] = jnp.where(ev_z, faces[0], faces[1])

    if send is not None:
        for k in range(chunks):
            lo, hi = p[0, at(k), :], p[cells_x - 1, at(k), :]
            send[0][at(k), :] = jnp.where(ev_x, hi, lo).astype(BF16)
            send[1][at(k), :] = jnp.where(ev_x, lo, hi).astype(BF16)


def fix_and_send(p_in, xe_in, xo_in, ze_in, zo_in, gx, gz, p, xe, xo, ze, zo):
    add_borders(p_in, xe_in, xo_in, ze_in, zo_in, gx, gz, p, (xe, xo, ze, zo))


def inner_part(ref, count):
    return ref.at[pl.ds(1, count), pl.ds(SUB, ref.shape[1] - 2 * SUB), :]


def border_parts(ref, count):
    cells_x, cells_z, _ = ref.shape
    planes = pl.ds(1, count)
    return [
        ref.at[0],
        ref.at[pl.ds(count + 1, cells_x - count - 1)],
        ref.at[planes, pl.ds(0, SUB), :],
        ref.at[planes, pl.ds(cells_z - SUB, SUB), :],
    ]


def early_planes(cells_x):
    return max(1, cells_x * 3 // 4 - 1)


def last_sweep(p, cx, cz, cy, inverse, rhs, out, out_h, sem):
    count = early_planes(p.shape[0])
    copy = pltpu.make_async_copy(inner_part(out, count), inner_part(out_h, count), sem)
    sweep(p, cx, cz, cy, inverse, lambda x, at: rhs[x, at, :], out, stop=count + 1)
    copy.start()
    sweep(p, cx, cz, cy, inverse, lambda x, at: rhs[x, at, :], out, start=count + 1)
    copy.wait()


def fix_and_gather(
    capacity, p_in, xe_in, xo_in, ze_in, zo_in, gx, gz, row_v, out_in, p, back, out_h, split, rows32, row, sem, sems
):
    del out_in
    cells_x, cells_z, beam = p.shape
    row_copy = pltpu.make_async_copy(row_v, row, sem)
    row_copy.start()
    add_borders(p_in, xe_in, xo_in, ze_in, zo_in, gx, gz, p)
    count = early_planes(cells_x)
    outs = fetch(border_parts(p, count), border_parts(out_h, count), sems)
    blocks = beam // LANES
    devices = back.shape[0]

    @pl.loop(0, cells_x)
    def _(x):
        for b, lanes in by_lanes(p):
            first = pl.multiple_of((x * blocks + b) * cells_z, SUB)
            split[pl.ds(first, cells_z), :] = p[x, :, lanes]

    row_copy.wait()

    @pl.loop(0, devices)
    def _(d):
        for s in range(capacity):
            rows32[pl.ds(d * capacity + s, 1), :] = split[pl.ds(row[d, s], 1), :]

    back[...] = rows32[...].astype(BF16).reshape(back.shape)
    for copy in outs:
        copy.wait()


def leave(back, slot, out):
    rows = back.shape[0] * back.shape[1]
    panels = out.shape[0]
    pick = lax.broadcasted_iota(jnp.int32, (rows, panels), 0) == slot[...]
    out[...] = lax.dot_general(
        jnp.where(pick, 1.0, 0.0).astype(BF16),
        back[...].reshape(rows, LANES),
        (((0,), (0,)), ((), ())),
        preferred_element_type=F32,
    ).astype(BF16)


def body(alpha, vel_x, vel_z, divergence, press_guess, panel_records, panel_dest, panel_segment):
    devices = lax.axis_size("slab") * lax.axis_size("depth")
    panels = panel_records.shape[0]
    capacity = 2 * panels // devices
    cells_x, cells_z, beam = alpha.shape
    field = shape(alpha.shape)
    rows = -(-(capacity + 1) // SUB) * SUB
    axes = ("slab", "depth")

    xs, zs = (cells_z, beam), (cells_x, beam)
    tile = (cells_x, SUB, beam)
    faces = [shape(xs, BF16)] * 2 + [shape(zs)] * 2
    two_faces = [shape((2,) + xs, BF16)] * 2 + [shape((2,) + zs)] * 2
    parts = len(parts_of(cells_x))
    lines = (cells_x * cells_z * beam // LANES, LANES)

    def near(dims, dtype=F32):
        return pltpu.VMEM(tuple(dims), dtype)

    def swaps(xe, xo, ze, zo):
        return swap(xe, "slab", 0), swap(xo, "slab", 1), swap(ze, "depth", 0), swap(zo, "depth", 1)

    *packed, send, slot = call(
        functools.partial(enter, capacity, rows, devices),
        faces + [shape((devices, rows, LANES), BF16), shape((1, panels), jnp.int32)],
        alpha, vel_x, vel_z,
        panel_dest.reshape(1, panels), panel_segment.reshape(1, panels), panel_records,
        far_in=(0, 1, 2, 3, 4, 5), far_out=(4, 5),
        scratch=[
            near(xs), near(xs), near(tile), near(tile), near(xs), near(tile),
            near((1, panels), jnp.int32),
            near((1, panels), jnp.int32),
            near((panels, LANES), BF16),
            near((1, panels), jnp.int32),
            near((devices, rows, LANES), BF16),
            DMA((11,)),
        ],
    )
    halo = swaps(*packed)
    got = lax.all_to_all(send, axes, split_axis=0, concat_axis=0, tiled=True)
    alpha_next, *packed = call(
        advect, [field] + two_faces, alpha, vel_x, vel_z, press_guess, *halo,
        far_in=(0, 1, 2, 3), far_out=(0,),
        scratch=[near(alpha.shape)] * 4 + [near(xs), near(xs), near(tile), near(tile), DMA((4, parts)), DMA((4,))],
    )
    halo = swaps(*packed)
    half, cx, cz, cy, inverse, rhs, pressure, row = call(
        functools.partial(middle, capacity),
        [field, shape((cells_x + 1,) + xs), field, field, field, field, field, shape((devices, LANES), jnp.int32)],
        got, alpha_next, divergence, press_guess,
        far_in=(1, 2, 3),
        scratch=[
            near((devices * rows, LANES)),
            near((devices, LANES), jnp.int32),
            pltpu.SMEM((devices, LANES), jnp.int32),
            near(lines),
            near(alpha.shape),
            near(alpha.shape),
            DMA((4,)),
            DMA,
        ],
    )
    pressure, inverse, gx, gz, *packed = call(
        close,
        [field, field, shape((2,) + xs), shape((2,) + zs)] + faces,
        pressure, inverse, half, *halo,
        aliases={0: 0, 1: 1},
        scratch=[near((2,) + xs)],
    )
    halo = swaps(*packed)
    (pressure,) = call(next_sweep, [field], pressure, cx, cz, cy, inverse, rhs)
    pressure, *packed = call(fix_and_send, [field] + faces, pressure, *halo, gx, gz, aliases={0: 0})
    halo = swaps(*packed)
    last, out = call(last_sweep, [field, field], pressure, cx, cz, cy, inverse, rhs, far_out=(1,), scratch=[DMA])
    _, back, pressure = call(
        functools.partial(fix_and_gather, capacity),
        [field, shape((devices, capacity, LANES), BF16), field],
        last, *halo, gx, gz, row, out,
        far_in=(8,), far_out=(2,),
        aliases={0: 0, 8: 2},
        scratch=[
            near(lines),
            near((devices * capacity, LANES)),
            pltpu.SMEM((devices, LANES), jnp.int32),
            DMA,
            DMA((4,)),
        ],
    )
    returned = lax.all_to_all(back, axes, split_axis=0, concat_axis=0, tiled=True)
    (panel_pressure,) = call(leave, [shape((panels, LANES), BF16)], returned, slot, free_out=(0,), limit=4 * MIB)
    return (pressure, alpha_next, panel_pressure)


def solution(mesh):
    in_specs = (
        P("slab", "depth", None),
        P("slab", "depth", None),
        P("slab", "depth", None),
        P("slab", "depth", None),
        P("slab", "depth", None),
        P(("slab", "depth"), None),
        P(("slab", "depth"), None),
        P(("slab", "depth"), None),
    )
    out_specs = (P("slab", "depth", None), P("slab", "depth", None), P(("slab", "depth"), None))
    return jax.shard_map(body, mesh=mesh, in_specs=in_specs, out_specs=out_specs, check_vma=False)
```

```python
import functools

import jax
import jax.numpy as jnp
from jax import lax
from jax.experimental import pallas as pl
from jax.experimental.pallas import tpu as pltpu
from jax.sharding import PartitionSpec as P


COURANT = 0.2
LANES = 128
SUB = 8
DIGIT = 256
MIB = 1 << 20
F32 = jnp.float32
BF16 = jnp.bfloat16

WHOLE = pl.BlockSpec(memory_space=pltpu.VMEM)
FAR = pl.BlockSpec(memory_space=pltpu.HBM)
DMA = pltpu.SemaphoreType.DMA


def call(kernel, outs, *args, aliases=None, far_in=(), far_out=(), free_out=(), in_specs=None, scratch=(), limit=12 * MIB):
    specs = [FAR if n in far_in else WHOLE for n in range(len(args))]
    for n, spec in (in_specs or {}).items():
        specs[n] = spec
    shapes = [o if n in far_out or n in free_out else pltpu.VMEM(o.shape, o.dtype) for n, o in enumerate(outs)]
    return pl.pallas_call(
        kernel,
        out_shape=shapes,
        in_specs=specs,
        out_specs=[FAR if n in far_out else WHOLE for n in range(len(outs))],
        scratch_shapes=list(scratch),
        input_output_aliases=aliases or {},
        compiler_params=pltpu.CompilerParams(vmem_limit_bytes=limit),
    )(*(pltpu.with_memory_space_constraint(a, pltpu.HBM) if n in far_in else a for n, a in enumerate(args)))


def shape(dims, dtype=F32):
    return jax.ShapeDtypeStruct(tuple(dims), dtype)


def even(axis):
    return lax.rem(lax.axis_index(axis), 2) == 0


def swap(block, axis, odd):
    slabs, depths = lax.axis_size("slab"), lax.axis_size("depth")
    pairs = []
    for i in range(slabs):
        for j in range(depths):
            own, count, other = (i, slabs, depths) if axis == "slab" else (j, depths, slabs)
            partner = own + 1 if own % 2 == odd else own - 1
            target = (partner, j) if axis == "slab" else (i, partner)
            if not 0 <= partner < count:
                if other % 2:
                    continue
                target = (i, j ^ 1) if axis == "slab" else (i ^ 1, j)
            pairs.append((i * depths + j, target[0] * depths + target[1]))
    return lax.ppermute(block, ("slab", "depth"), pairs)


def inner(axis):
    i = lax.axis_index(axis)
    return [jnp.where(i > 0, 1.0, 0.0), jnp.where(i < lax.axis_size(axis) - 1, 1.0, 0.0)]


def unrolled(begin, end, most=4):
    count = end - begin
    return pl.loop(begin, end, unroll=next(n for n in range(most, 0, -1) if count % n == 0))


def row_is(rows, index):
    return lax.broadcasted_iota(jnp.int32, rows, 0) == index


def z_tiles(ref):
    last = ref.shape[1] // SUB - 1
    return [ref.at[:, pl.ds(0, SUB), :], ref.at[:, pl.ds(last * SUB, SUB), :]]


def x_planes(ref):
    return [ref.at[0], ref.at[ref.shape[0] - 1]]


def fetch(sources, targets, sems):
    copies = []
    for n, (source, target) in enumerate(zip(sources, targets)):
        copies.append(pltpu.make_async_copy(source, target, sems.at[n]))
        copies[-1].start()
    return copies


def pack_first(a0, a1, az0, az1, vx0, vz0, xe, xo, ze, zo):
    ev_x = even("slab")
    ev_z = even("depth")

    def fold(v, a):
        return jnp.where(v > 0, v, v * a)

    for k in range(a0.shape[0] // SUB):
        at = pl.ds(k * SUB, SUB)
        up = a1[at, :]
        down = fold(vx0[at, :], a0[at, :])
        xe[at, :] = jnp.where(ev_x, up, down).astype(BF16)
        xo[at, :] = jnp.where(ev_x, down, up).astype(BF16)
    for x in range(az0.shape[0]):
        up = az1[x, SUB - 1:SUB, :]
        down = fold(vz0[x, 0:1, :], az0[x, 0:1, :])
        ze[x:x + 1, :] = jnp.where(ev_z, up, down)
        zo[x:x + 1, :] = jnp.where(ev_z, down, up)


def enter(
    capacity, rows, devices,
    alpha, vx, vz, dest_h, seg_h, rec_h,
    xe, xo, ze, zo, send_h, slot_h,
    a0, a1, az0, az1, vx0, vz0, dest, seg, rec, slot_v, send, sems,
):
    sources = x_planes(alpha) + z_tiles(alpha) + x_planes(vx)[:1] + z_tiles(vz)[:1]
    borders = [a0, a1, az0, az1, vx0, vz0]
    copies = fetch([dest_h, seg_h, rec_h] + sources, [dest, seg, rec] + borders, sems)
    panels = dest.shape[1]
    copies[0].wait()
    copies[1].wait()
    d = dest[...]
    s = seg[...]
    hot = lax.broadcasted_iota(jnp.int32, (devices, panels), 0) == d
    hot_f = jnp.where(hot, 1.0, 0.0)
    before_me = lax.broadcasted_iota(jnp.int32, (panels, panels), 0) < lax.broadcasted_iota(
        jnp.int32, (panels, panels), 1
    )
    before = jnp.dot(
        hot_f.astype(BF16), jnp.where(before_me, 1.0, 0.0).astype(BF16), preferred_element_type=F32
    )
    slot = jnp.sum(before * hot_f, axis=0, keepdims=True).astype(jnp.int32)
    slot_v[...] = d * capacity + slot
    slot_out = pltpu.make_async_copy(slot_v, slot_h, sems.at[9])
    slot_out.start()
    place = d * rows + slot
    pick = lax.broadcasted_iota(jnp.int32, (devices * rows, panels), 0) == place
    copies[2].wait()
    records = jnp.dot(jnp.where(pick, 1.0, 0.0).astype(BF16), rec[...], preferred_element_type=F32)
    high = (s // DIGIT + 1).astype(F32)
    low = (s % DIGIT).astype(F32)
    lane = lax.broadcasted_iota(jnp.int32, (LANES, panels), 0)
    at_high = jnp.where(lane == slot, 1.0, 0.0).astype(BF16)
    at_low = jnp.where(lane == slot + capacity, 1.0, 0.0).astype(BF16)
    contract = (((1,), (1,)), ((), ()))
    digits = lax.dot_general(
        (hot_f * high).astype(BF16), at_high, contract, preferred_element_type=F32
    ) + lax.dot_general((hot_f * low).astype(BF16), at_low, contract, preferred_element_type=F32)
    digits = jnp.broadcast_to(digits[:, None, :], (devices, rows, LANES)).reshape(devices * rows, LANES)
    is_digit = lax.rem(lax.broadcasted_iota(jnp.int32, records.shape, 0), rows) >= capacity
    send[...] = jnp.where(is_digit, digits, records).astype(BF16)
    send_out = pltpu.make_async_copy(send, send_h, sems.at[10])
    send_out.start()
    for copy in copies[3:]:
        copy.wait()
    pack_first(*borders, xe, xo, ze, zo)
    slot_out.wait()
    send_out.wait()


def parts_of(cells_x):
    step = max(1, cells_x // 8)
    return [(first, min(step, cells_x - first)) for first in range(0, cells_x, step)]


def fetch_fields(fields, sems):
    copies = [[] for _ in fields]
    for n, (first, count) in enumerate(parts_of(fields[0][1].shape[0])):
        planes = pl.ds(first, count)
        for row, (source, target) in enumerate(fields):
            copy = pltpu.make_async_copy(source.at[planes], target.at[planes], sems.at[row, n])
            copy.start()
            copies[row].append(copy)
    return copies


def advect(
    alpha, vx_h, vz_h, p_h, xe_in, xo_in, ze_in, zo_in,
    out_h, early, xe, xo, ze, zo,
    vx, vz, out, p0, p1, pz0, pz1, sems, p_sems,
):
    cells_x, cells_z, beam = alpha.shape
    chunks = cells_z // SUB
    ev_x = even("slab")
    ev_z = even("depth")
    top = row_is((SUB, beam), 0)
    bottom = row_is((SUB, beam), SUB - 1)
    parts = parts_of(cells_x)
    fields = ((vx_h, vx), (vz_h, vz))
    ins = fetch_fields(fields, sems)
    p_ins = fetch(x_planes(p_h) + z_tiles(p_h), [p0, p1, pz0, pz1], p_sems)
    outs = [
        pltpu.make_async_copy(out.at[pl.ds(f, c)], out_h.at[pl.ds(f, c)], sems.at[len(fields), n])
        for n, (f, c) in enumerate(parts)
    ]

    def at(k):
        return pl.ds(k * SUB, SUB)

    has_x, has_z = inner("slab"), inner("depth")

    def plane(x, first, last):
        zlo = has_z[0] * jnp.where(ev_z, zo_in[pl.ds(x, 1), :], ze_in[pl.ds(x, 1), :])
        zhi = has_z[1] * jnp.where(ev_z, ze_in[pl.ds(x, 1), :], zo_in[pl.ds(x, 1), :])
        above = None
        for k in reversed(range(chunks)):
            a = alpha[x, at(k), :]
            v = vx[x, at(k), :]
            if first:
                am = has_x[0] * jnp.where(ev_x, xo_in[at(k), :], xe_in[at(k), :]).astype(F32)
            else:
                am = alpha[x - 1, at(k), :]
            fx = v * jnp.where(v > 0, am, a)
            if last:
                q = has_x[1] * jnp.where(ev_x, xe_in[at(k), :], xo_in[at(k), :]).astype(F32)
                fxn = jnp.where(q > 0, q * a, q)
            else:
                vn = vx[x + 1, at(k), :]
                fxn = vn * jnp.where(vn > 0, a, alpha[x + 1, at(k), :])
            w = vz[x, at(k), :]
            if k == 0:
                edge = jnp.broadcast_to(zlo, a.shape)
            else:
                edge = pltpu.roll(alpha[x, at(k - 1), :], 1, 0)
            ad = jnp.where(top, edge, pltpu.roll(a, 1, 0))
            fz = w * jnp.where(w > 0, ad, a)
            up = pltpu.roll(fz, SUB - 1, 0)
            if above is None:
                q = jnp.broadcast_to(zhi, a.shape)
                fzn = jnp.where(bottom, jnp.where(q > 0, q * a, q), up)
            else:
                fzn = jnp.where(bottom, above, up)
            above = up
            new = a - COURANT * (fxn - fx + fzn - fz)
            out[x, at(k), :] = new
            if k == chunks - 1:
                z_up = new[SUB - 1:SUB, :] - 0.5
            if k == 0:
                z_down = new[0:1, :] - 0.5
        ze[0, pl.ds(x, 1), :] = jnp.where(ev_z, z_up, z_down)
        zo[0, pl.ds(x, 1), :] = jnp.where(ev_z, z_down, z_up)

    for n, (first, count) in enumerate(parts):
        for copies in ins:
            copies[n].wait()
        begin = max(first - 1, 0)
        end = first + count - 1
        if begin == 0:
            plane(0, True, end == begin and cells_x == 1)
            begin = 1

        @pl.loop(begin, end)
        def _(x):
            plane(x, False, False)

        if n == len(parts) - 1:
            plane(cells_x - 1, False, True)
        if n > 0:
            outs[n - 1].start()
    outs[-1].start()
    early[...] = out[pl.ds(0, early.shape[0])]

    for copy in p_ins:
        copy.wait()
    for k in range(chunks):
        for which, up, down in ((0, out[cells_x - 1, at(k), :] - 0.5, out[0, at(k), :] - 0.5), (1, p1[at(k), :], p0[at(k), :])):
            xe[which, at(k), :] = jnp.where(ev_x, up, down).astype(BF16)
            xo[which, at(k), :] = jnp.where(ev_x, down, up).astype(BF16)
    for x in range(cells_x):
        up = pz1[x, SUB - 1:SUB, :]
        down = pz0[x, 0:1, :]
        ze[1, x:x + 1, :] = jnp.where(ev_z, up, down)
        zo[1, x:x + 1, :] = jnp.where(ev_z, down, up)
    for copy in outs:
        copy.wait()


def coefficients(half, cx, cz, cy, inverse, arrived):
    cells_x, cells_z, beam = half.shape
    chunks = cells_z // SUB
    top = row_is((SUB, beam), 0)
    bottom = row_is((SUB, beam), SUB - 1)
    lane = lax.broadcasted_iota(jnp.int32, (SUB, LANES), 1)
    start_lane, end_lane = lane == 0, lane == LANES - 1
    none = jnp.zeros((cells_z, beam), F32)
    cx[0] = none
    cx[cells_x] = none

    def at(k):
        return pl.ds(k * SUB, SUB)

    def first_lane_zero(v):
        return jnp.concatenate([jnp.where(start_lane, 0.0, v[:, :LANES]), v[:, LANES:]], axis=1)

    def plane(x, last):
        above = jnp.zeros((SUB, beam), F32)
        rolled = pltpu.roll(half[x, at(chunks - 1), :], 1, 0)
        for k in reversed(range(chunks)):
            r = half[x, at(k), :]
            total = cx[x, at(k), :]
            if not last:
                hx = 1.0 / (r + half[x + 1, at(k), :])
                cx[x + 1, at(k), :] = hx
                total = total + hx
            if k == 0:
                hz = jnp.where(top, 0.0, 1.0 / (r + rolled))
            else:
                below = pltpu.roll(half[x, at(k - 1), :], 1, 0)
                hz = 1.0 / (r + jnp.where(top, below, rolled))
                rolled = below
            cz[x, at(k), :] = hz
            up = pltpu.roll(hz, SUB - 1, 0)
            total = total + (hz + jnp.where(bottom, above, up))
            above = up
            hy_all = 1.0 / (r + first_lane_zero(pltpu.roll(r, 1, 1)))
            hy = first_lane_zero(hy_all)
            cy[x, at(k), :] = hy
            edge = jnp.where(end_lane, 1.0 / r[:, beam - LANES:], 0.0)
            hy_up = pltpu.roll(hy, beam - 1, 1)
            hy_up = jnp.concatenate(
                [hy_up[:, : beam - LANES], hy_up[:, beam - LANES:] + edge], axis=1
            )
            inverse[x, at(k), :] = 1.0 / (total + (hy_all + hy_up))

    begin = 0
    for stop in arrived():
        @unrolled(begin, stop - 1, 1)
        def _(x):
            plane(x, False)

        begin = stop - 1
    plane(cells_x - 1, True)


def close(
    p_in, inverse_in, half, xe_in, xo_in, ze_in, zo_in,
    p, inverse, gx, gz, xe, xo, ze, zo,
    wx,
):
    del p_in, inverse_in
    cells_x, cells_z, beam = half.shape
    chunks = cells_z // SUB
    ev_x, ev_z = even("slab"), even("depth")
    has = [inner("slab"), inner("depth")]

    def at(k):
        return pl.ds(k * SUB, SUB)

    for side, x in ((0, 0), (1, cells_x - 1)):
        for k in range(chunks):
            a, b = xe_in[:, at(k), :], xo_in[:, at(k), :]
            v = (jnp.where(ev_x, a, b) if side else jnp.where(ev_x, b, a)).astype(F32)
            halo = has[0][side] * (4.5 * v[0] + 2.75)
            c = 1.0 / (half[x, at(k), :] + halo)
            w = 1.0 / inverse[x, at(k), :]
            open_c = has[0][side] * c
            p[x, at(k), :] = p[x, at(k), :] * w + open_c * v[1]
            gx[side, at(k), :] = open_c
            wx[side, at(k), :] = w + c

    def rows(x, plane):
        faces = []
        for side, k in ((0, 0), (1, chunks - 1)):
            here = row_is((SUB, beam), 0 if side == 0 else SUB - 1)
            a, b = ze_in[:, pl.ds(x, 1), :], zo_in[:, pl.ds(x, 1), :]
            v = jnp.where(ev_z, a, b) if side else jnp.where(ev_z, b, a)
            halo = jnp.broadcast_to(has[1][side] * (4.5 * v[0] + 2.75), (SUB, beam))
            c = jnp.where(here, 1.0 / (half[x, at(k), :] + halo), 0.0)
            open_c = has[1][side] * c
            add = open_c * jnp.broadcast_to(v[1], (SUB, beam))
            if plane is None:
                w = 1.0 / inverse[x, at(k), :]
                total = p[x, at(k), :] * w + add
                inv = 1.0 / (w + c)
                inverse[x, at(k), :] = inv
                new = total * inv
                p[x, at(k), :] = new
            else:
                w = wx[plane, at(k), :] + c
                wx[plane, at(k), :] = w
                inv = 1.0 / w
                total = p[x, at(k), :] + add
                p[x, at(k), :] = total
                new = total * inv
            g = inv * open_c
            r = slice(0, 1) if side == 0 else slice(SUB - 1, SUB)
            gz[side, pl.ds(x, 1), :] = g[r, :]
            faces.append(new[r, :])
        ze[pl.ds(x, 1), :] = jnp.where(ev_z, faces[1], faces[0])
        zo[pl.ds(x, 1), :] = jnp.where(ev_z, faces[0], faces[1])

    rows(0, 0)
    rows(cells_x - 1, 1)

    @pl.loop(1, cells_x - 1)
    def _(x):
        rows(x, None)

    for k in range(chunks):
        new = []
        for side, x in ((0, 0), (1, cells_x - 1)):
            inv = 1.0 / wx[side, at(k), :]
            inverse[x, at(k), :] = inv
            gx[side, at(k), :] = gx[side, at(k), :] * inv
            new.append(p[x, at(k), :] * inv)
            p[x, at(k), :] = new[side]
        xe[at(k), :] = jnp.where(ev_x, new[1], new[0]).astype(BF16)
        xo[at(k), :] = jnp.where(ev_x, new[0], new[1]).astype(BF16)


def by_lanes(ref):
    _, _, beam = ref.shape
    blocks = beam // LANES
    for b in range(blocks):
        yield b, pl.ds(b * LANES, LANES)


def middle(
    capacity, rows, got, early, alpha_h, div_h, p_h,
    half, cx, cz, cy, inverse, rhs, p, row_out,
    hull, div, p0, rec32, row_v, row_s, sems, sem,
):
    devices = got.shape[0] // rows
    cells_x, cells_z, beam = rhs.shape
    blocks = beam // LANES
    rec32[...] = got[...].astype(F32)
    digits = rec32[pl.ds(rows - 1, devices, stride=rows), :]
    seg = (digits * float(DIGIT) + pltpu.roll(digits, LANES - capacity, 1)).astype(jnp.int32) - DIGIT
    across = seg // blocks
    row = ((across // cells_z) * blocks + seg % blocks) * cells_z + across % cells_z
    slots = lax.broadcasted_iota(jnp.int32, seg.shape, 0) * capacity
    slots = slots + lax.broadcasted_iota(jnp.int32, seg.shape, 1)
    row = jnp.where(seg < 0, slots % hull.shape[0], row)
    row_v[...] = row
    copy = pltpu.make_async_copy(row_v, row_s, sem)
    copy.start()
    per = LANES // capacity
    lane = lax.broadcasted_iota(jnp.int32, (devices // per, LANES), 1)
    table = jnp.zeros(lane.shape, jnp.int32)
    for j in range(per):
        piece = pltpu.roll(row_v[pl.ds(j, devices // per, stride=per), :], j * capacity, 1)
        table = jnp.where(lane // capacity == j, piece, table)
    row_out[pl.ds(0, devices // per)] = table
    cut = early.shape[0]
    late = pl.ds(cut, cells_x - cut)
    alpha_in = pltpu.make_async_copy(alpha_h.at[late], half.at[late], sems.at[0])
    alpha_in.start()
    rest = [
        pltpu.make_async_copy(h, v, sems.at[1 + n]) for n, (h, v) in enumerate(((div_h, div), (p_h, p0)))
    ]
    for other in rest:
        other.start()

    def arrived():
        half[pl.ds(0, cut)] = 0.5 + 4.5 * early[...]
        yield cut
        hull[...] = jnp.zeros_like(hull)
        alpha_in.wait()

        @unrolled(cut, cells_x)
        def _(x):
            half[x] = 0.5 + 4.5 * half[x]

        yield cells_x

    coefficients(half, cx, cz, cy, inverse, arrived)
    copy.wait()

    @pl.loop(0, devices)
    def _(d):
        for s in range(capacity):
            hull[pl.ds(row_s[d, s], 1), :] += rec32[pl.ds(d * rows + s, 1), :]

    for other in rest:
        other.wait()

    def source(x, at):
        parts = []
        for b, lanes in by_lanes(rhs):
            first = pl.multiple_of((x * blocks + b) * cells_z + at.start, SUB)
            parts.append(div[x, at, lanes] + hull[pl.ds(first, SUB), :])
        value = jnp.concatenate(parts, axis=1)
        rhs[x, at, :] = value
        return value

    sweep(p0, cx, cz, cy, inverse, source, p)


def sweep(p, cx, cz, cy, inverse, source, out, start=0, stop=None):
    cells_x, cells_z, beam = p.shape
    chunks = cells_z // SUB
    top = row_is((SUB, beam), 0)
    bottom = row_is((SUB, beam), SUB - 1)

    def at(k):
        return pl.ds(k * SUB, SUB)

    @unrolled(start, cells_x if stop is None else stop)
    def _(x):
        prv = jnp.maximum(x - 1, 0)
        nxt = jnp.minimum(x + 1, cells_x - 1)
        above = jnp.zeros((SUB, beam), F32)
        rolled = pltpu.roll(p[x, at(chunks - 1), :], 1, 0)
        for k in reversed(range(chunks)):
            here = p[x, at(k), :]
            hz = cz[x, at(k), :]
            hy = cy[x, at(k), :]
            total = cx[x, at(k), :] * p[prv, at(k), :] + cx[x + 1, at(k), :] * p[nxt, at(k), :]
            if k > 0:
                below = pltpu.roll(p[x, at(k - 1), :], 1, 0)
                down = jnp.where(top, below, rolled)
                rolled = below
            else:
                down = rolled
            up = pltpu.roll(hz * here, SUB - 1, 0)
            total = total + (hz * down + jnp.where(bottom, above, up))
            above = up
            total = total + (hy * pltpu.roll(here, 1, 1) + pltpu.roll(hy * here, beam - 1, 1))
            out[x, at(k), :] = (total - source(x, at(k))) * inverse[x, at(k), :]


def next_sweep(p, cx, cz, cy, inverse, rhs, out):
    sweep(p, cx, cz, cy, inverse, lambda x, at: rhs[x, at, :], out)


def add_borders(p_in, xe_in, xo_in, ze_in, zo_in, gx, gz, p, send=None):
    del p_in
    cells_x, cells_z, beam = p.shape
    chunks = cells_z // SUB
    ev_x, ev_z = even("slab"), even("depth")

    def at(k):
        return pl.ds(k * SUB, SUB)

    for side, x in ((0, 0), (1, cells_x - 1)):
        for k in range(chunks):
            a, b = xe_in[at(k), :], xo_in[at(k), :]
            v = jnp.where(ev_x, a, b) if side else jnp.where(ev_x, b, a)
            p[x, at(k), :] = p[x, at(k), :] + gx[side, at(k), :] * v.astype(F32)

    @pl.loop(0, cells_x)
    def _(x):
        faces = []
        for side, k in ((0, 0), (1, chunks - 1)):
            here = row_is((SUB, beam), 0 if side == 0 else SUB - 1)
            a, b = ze_in[pl.ds(x, 1), :], zo_in[pl.ds(x, 1), :]
            v = jnp.where(ev_z, a, b) if side else jnp.where(ev_z, b, a)
            add = jnp.broadcast_to(gz[side, pl.ds(x, 1), :] * v, (SUB, beam))
            new = p[x, at(k), :] + jnp.where(here, add, 0.0)
            p[x, at(k), :] = new
            faces.append(new[0:1, :] if side == 0 else new[SUB - 1:SUB, :])
        if send is not None:
            send[2][pl.ds(x, 1), :] = jnp.where(ev_z, faces[1], faces[0])
            send[3][pl.ds(x, 1), :] = jnp.where(ev_z, faces[0], faces[1])

    if send is not None:
        for k in range(chunks):
            lo, hi = p[0, at(k), :], p[cells_x - 1, at(k), :]
            send[0][at(k), :] = jnp.where(ev_x, hi, lo).astype(BF16)
            send[1][at(k), :] = jnp.where(ev_x, lo, hi).astype(BF16)


def fix_and_send(p_in, xe_in, xo_in, ze_in, zo_in, gx, gz, p, xe, xo, ze, zo):
    add_borders(p_in, xe_in, xo_in, ze_in, zo_in, gx, gz, p, (xe, xo, ze, zo))


def inner_part(ref, count):
    return ref.at[pl.ds(1, count), pl.ds(SUB, ref.shape[1] - 2 * SUB), :]


def border_parts(ref, count):
    cells_x, cells_z, _ = ref.shape
    planes = pl.ds(1, count)
    return [
        ref.at[0],
        ref.at[pl.ds(count + 1, cells_x - count - 1)],
        ref.at[planes, pl.ds(0, SUB), :],
        ref.at[planes, pl.ds(cells_z - SUB, SUB), :],
    ]


def early_planes(cells_x):
    return max(1, cells_x * 3 // 4 - 1)


def last_sweep(p, cx, cz, cy, inverse, rhs, out, out_h, sem):
    count = early_planes(p.shape[0])
    copy = pltpu.make_async_copy(inner_part(out, count), inner_part(out_h, count), sem)
    sweep(p, cx, cz, cy, inverse, lambda x, at: rhs[x, at, :], out, stop=count + 1)
    copy.start()
    sweep(p, cx, cz, cy, inverse, lambda x, at: rhs[x, at, :], out, start=count + 1)
    copy.wait()


def fix_and_gather(
    p_in, xe_in, xo_in, ze_in, zo_in, gx, gz, row_v, out_in, p, back, out_h, split, rows32, row, sem, sems
):
    del out_in
    cells_x, cells_z, beam = p.shape
    row_copy = pltpu.make_async_copy(row_v.at[pl.ds(0, row.shape[0])], row, sem)
    row_copy.start()
    add_borders(p_in, xe_in, xo_in, ze_in, zo_in, gx, gz, p)
    count = early_planes(cells_x)
    outs = fetch(border_parts(p, count), border_parts(out_h, count), sems)
    blocks = beam // LANES

    @pl.loop(0, cells_x)
    def _(x):
        for b, lanes in by_lanes(p):
            first = pl.multiple_of((x * blocks + b) * cells_z, SUB)
            split[pl.ds(first, cells_z), :] = p[x, :, lanes]

    row_copy.wait()

    @pl.loop(0, row.shape[0])
    def _(g):
        for lane in range(LANES):
            rows32[pl.ds(g * LANES + lane, 1), :] = split[pl.ds(row[g, lane], 1), :]

    back[...] = rows32[...].astype(BF16).reshape(back.shape)
    for copy in outs:
        copy.wait()


def leave(back, slot, out):
    rows = back.shape[0] * back.shape[1]
    panels = out.shape[0]
    pick = lax.broadcasted_iota(jnp.int32, (rows, panels), 0) == slot[...]
    out[...] = lax.dot_general(
        jnp.where(pick, 1.0, 0.0).astype(BF16),
        back[...].reshape(rows, LANES),
        (((0,), (0,)), ((), ())),
        preferred_element_type=F32,
    ).astype(BF16)


def body(alpha, vel_x, vel_z, divergence, press_guess, panel_records, panel_dest, panel_segment):
    devices = lax.axis_size("slab") * lax.axis_size("depth")
    panels = panel_records.shape[0]
    capacity = 2 * panels // devices
    cells_x, cells_z, beam = alpha.shape
    field = shape(alpha.shape)
    rows = (capacity + 2) // 2 * 2
    axes = ("slab", "depth")

    xs, zs = (cells_z, beam), (cells_x, beam)
    tile = (cells_x, SUB, beam)
    faces = [shape(xs, BF16)] * 2 + [shape(zs)] * 2
    two_faces = [shape((2,) + xs, BF16)] * 2 + [shape((2,) + zs)] * 2
    parts = len(parts_of(cells_x))
    table = (devices * capacity // LANES, LANES)
    lines = (cells_x * cells_z * beam // LANES, LANES)

    def near(dims, dtype=F32):
        return pltpu.VMEM(tuple(dims), dtype)

    def swaps(xe, xo, ze, zo):
        return swap(xe, "slab", 0), swap(xo, "slab", 1), swap(ze, "depth", 0), swap(zo, "depth", 1)

    *packed, send, slot = call(
        functools.partial(enter, capacity, rows, devices),
        faces + [shape((devices * rows, LANES), BF16), shape((1, panels), jnp.int32)],
        alpha, vel_x, vel_z,
        panel_dest.reshape(1, panels), panel_segment.reshape(1, panels), panel_records,
        far_in=(0, 1, 2, 3, 4, 5), far_out=(4, 5),
        scratch=[
            near(xs), near(xs), near(tile), near(tile), near(xs), near(tile),
            near((1, panels), jnp.int32),
            near((1, panels), jnp.int32),
            near((panels, LANES), BF16),
            near((1, panels), jnp.int32),
            near((devices * rows, LANES), BF16),
            DMA((11,)),
        ],
    )
    halo = swaps(*packed)
    got = lax.all_to_all(
        send.reshape(devices, rows // 2, 2, LANES), axes, split_axis=0, concat_axis=0, tiled=True
    ).reshape(devices * rows, LANES)
    cut = max(1, cells_x // 4)
    alpha_next, early, *packed = call(
        advect, [field, shape((cut,) + xs)] + two_faces, alpha, vel_x, vel_z, press_guess, *halo,
        far_in=(1, 2, 3), far_out=(0,),
        scratch=[near(alpha.shape)] * 3 + [near(xs), near(xs), near(tile), near(tile), DMA((4, parts)), DMA((4,))],
    )
    halo = swaps(*packed)
    half, cx, cz, cy, inverse, rhs, pressure, row = call(
        functools.partial(middle, capacity, rows),
        [field, shape((cells_x + 1,) + xs), field, field, field, field, field, shape((devices, LANES), jnp.int32)],
        got, early, alpha_next, divergence, press_guess,
        far_in=(2, 3, 4),
        scratch=[
            near(lines),
            near(alpha.shape),
            near(alpha.shape),
            near((devices * rows, LANES)),
            near((devices, LANES), jnp.int32),
            pltpu.SMEM((devices, LANES), jnp.int32),
            DMA((3,)),
            DMA,
        ],
    )
    pressure, inverse, gx, gz, *packed = call(
        close,
        [field, field, shape((2,) + xs), shape((2,) + zs)] + faces,
        pressure, inverse, half, *halo,
        aliases={0: 0, 1: 1},
        scratch=[near((2,) + xs)],
    )
    halo = swaps(*packed)
    (pressure,) = call(next_sweep, [field], pressure, cx, cz, cy, inverse, rhs)
    pressure, *packed = call(fix_and_send, [field] + faces, pressure, *halo, gx, gz, aliases={0: 0})
    halo = swaps(*packed)
    last, out = call(last_sweep, [field, field], pressure, cx, cz, cy, inverse, rhs, far_out=(1,), scratch=[DMA])
    _, back, pressure = call(
        fix_and_gather,
        [field, shape((devices, capacity, LANES), BF16), field],
        last, *halo, gx, gz, row, out,
        far_in=(8,), far_out=(2,),
        aliases={0: 0, 8: 2},
        scratch=[
            near(lines),
            near((devices * capacity, LANES)),
            pltpu.SMEM(table, jnp.int32),
            DMA,
            DMA((4,)),
        ],
    )
    returned = lax.all_to_all(back, axes, split_axis=0, concat_axis=0, tiled=True)
    (panel_pressure,) = call(leave, [shape((panels, LANES), BF16)], returned, slot, free_out=(0,), limit=4 * MIB)
    return (pressure, alpha_next, panel_pressure)


def solution(mesh):
    in_specs = (
        P("slab", "depth", None),
        P("slab", "depth", None),
        P("slab", "depth", None),
        P("slab", "depth", None),
        P("slab", "depth", None),
        P(("slab", "depth"), None),
        P(("slab", "depth"), None),
        P(("slab", "depth"), None),
    )
    out_specs = (P("slab", "depth", None), P("slab", "depth", None), P(("slab", "depth"), None))
    return jax.shard_map(body, mesh=mesh, in_specs=in_specs, out_specs=out_specs, check_vma=False)
```

```python
import functools

import jax
import jax.numpy as jnp
from jax import lax
from jax.experimental import pallas as pl
from jax.experimental.pallas import tpu as pltpu
from jax.sharding import PartitionSpec as P


COURANT = 0.2
LANES = 128
SUB = 8
DIGIT = 256
MIB = 1 << 20
F32 = jnp.float32
BF16 = jnp.bfloat16

WHOLE = pl.BlockSpec(memory_space=pltpu.VMEM)
FAR = pl.BlockSpec(memory_space=pltpu.HBM)
DMA = pltpu.SemaphoreType.DMA


def call(kernel, outs, *args, aliases=None, far_in=(), far_out=(), free_out=(), in_specs=None, scratch=(), limit=12 * MIB):
    specs = [FAR if n in far_in else WHOLE for n in range(len(args))]
    for n, spec in (in_specs or {}).items():
        specs[n] = spec
    shapes = [o if n in far_out or n in free_out else pltpu.VMEM(o.shape, o.dtype) for n, o in enumerate(outs)]
    return pl.pallas_call(
        kernel,
        out_shape=shapes,
        in_specs=specs,
        out_specs=[FAR if n in far_out else WHOLE for n in range(len(outs))],
        scratch_shapes=list(scratch),
        input_output_aliases=aliases or {},
        compiler_params=pltpu.CompilerParams(vmem_limit_bytes=limit),
    )(*(pltpu.with_memory_space_constraint(a, pltpu.HBM) if n in far_in else a for n, a in enumerate(args)))


def shape(dims, dtype=F32):
    return jax.ShapeDtypeStruct(tuple(dims), dtype)


def even(axis):
    return lax.rem(lax.axis_index(axis), 2) == 0


def swap(block, axis, odd):
    slabs, depths = lax.axis_size("slab"), lax.axis_size("depth")
    pairs = []
    for i in range(slabs):
        for j in range(depths):
            own, count, other = (i, slabs, depths) if axis == "slab" else (j, depths, slabs)
            partner = own + 1 if own % 2 == odd else own - 1
            target = (partner, j) if axis == "slab" else (i, partner)
            if not 0 <= partner < count:
                if other % 2:
                    continue
                target = (i, j ^ 1) if axis == "slab" else (i ^ 1, j)
            pairs.append((i * depths + j, target[0] * depths + target[1]))
    return lax.ppermute(block, ("slab", "depth"), pairs)


def inner(axis):
    i = lax.axis_index(axis)
    return [jnp.where(i > 0, 1.0, 0.0), jnp.where(i < lax.axis_size(axis) - 1, 1.0, 0.0)]


def unrolled(begin, end, most=4):
    count = end - begin
    return pl.loop(begin, end, unroll=next(n for n in range(most, 0, -1) if count % n == 0))


def row_is(rows, index):
    return lax.broadcasted_iota(jnp.int32, rows, 0) == index


def z_tiles(ref):
    last = ref.shape[1] // SUB - 1
    return [ref.at[:, pl.ds(0, SUB), :], ref.at[:, pl.ds(last * SUB, SUB), :]]


def x_planes(ref):
    return [ref.at[0], ref.at[ref.shape[0] - 1]]


def fetch(sources, targets, sems):
    copies = []
    for n, (source, target) in enumerate(zip(sources, targets)):
        copies.append(pltpu.make_async_copy(source, target, sems.at[n]))
        copies[-1].start()
    return copies


def pack_first(a0, a1, az0, az1, vx0, vz0, xe, xo, ze, zo):
    ev_x = even("slab")
    ev_z = even("depth")

    def fold(v, a):
        return jnp.where(v > 0, v, v * a)

    for k in range(a0.shape[0] // SUB):
        at = pl.ds(k * SUB, SUB)
        up = a1[at, :]
        down = fold(vx0[at, :], a0[at, :])
        xe[at, :] = jnp.where(ev_x, up, down).astype(BF16)
        xo[at, :] = jnp.where(ev_x, down, up).astype(BF16)
    for x in range(az0.shape[0]):
        up = az1[x, SUB - 1:SUB, :]
        down = fold(vz0[x, 0:1, :], az0[x, 0:1, :])
        ze[x:x + 1, :] = jnp.where(ev_z, up, down)
        zo[x:x + 1, :] = jnp.where(ev_z, down, up)


def enter(
    capacity, rows, devices,
    alpha, vx, vz, dest_h, seg_h, rec_h,
    xe, xo, ze, zo, send_h, slot_h,
    a0, a1, az0, az1, vx0, vz0, dest, seg, rec, slot_v, send, sems,
):
    sources = x_planes(alpha) + z_tiles(alpha) + x_planes(vx)[:1] + z_tiles(vz)[:1]
    borders = [a0, a1, az0, az1, vx0, vz0]
    copies = fetch([dest_h, seg_h, rec_h] + sources, [dest, seg, rec] + borders, sems)
    panels = dest.shape[1]
    copies[0].wait()
    copies[1].wait()
    d = dest[...]
    s = seg[...]
    hot = lax.broadcasted_iota(jnp.int32, (devices, panels), 0) == d
    hot_f = jnp.where(hot, 1.0, 0.0)
    before_me = lax.broadcasted_iota(jnp.int32, (panels, panels), 0) < lax.broadcasted_iota(
        jnp.int32, (panels, panels), 1
    )
    before = jnp.dot(
        hot_f.astype(BF16), jnp.where(before_me, 1.0, 0.0).astype(BF16), preferred_element_type=F32
    )
    slot = jnp.sum(before * hot_f, axis=0, keepdims=True).astype(jnp.int32)
    slot_v[...] = d * capacity + slot
    slot_out = pltpu.make_async_copy(slot_v, slot_h, sems.at[9])
    slot_out.start()
    place = d * rows + slot
    pick = lax.broadcasted_iota(jnp.int32, (devices * rows, panels), 0) == place
    copies[2].wait()
    records = jnp.dot(jnp.where(pick, 1.0, 0.0).astype(BF16), rec[...], preferred_element_type=F32)
    high = (s // DIGIT + 1).astype(F32)
    low = (s % DIGIT).astype(F32)
    lane = lax.broadcasted_iota(jnp.int32, (LANES, panels), 0)
    at_high = jnp.where(lane == slot, 1.0, 0.0).astype(BF16)
    at_low = jnp.where(lane == slot + capacity, 1.0, 0.0).astype(BF16)
    contract = (((1,), (1,)), ((), ()))
    digits = lax.dot_general(
        (hot_f * high).astype(BF16), at_high, contract, preferred_element_type=F32
    ) + lax.dot_general((hot_f * low).astype(BF16), at_low, contract, preferred_element_type=F32)
    digits = jnp.broadcast_to(digits[:, None, :], (devices, rows, LANES)).reshape(devices * rows, LANES)
    is_digit = lax.rem(lax.broadcasted_iota(jnp.int32, records.shape, 0), rows) >= capacity
    send[...] = jnp.where(is_digit, digits, records).astype(BF16)
    send_out = pltpu.make_async_copy(send, send_h, sems.at[10])
    send_out.start()
    for copy in copies[3:]:
        copy.wait()
    pack_first(*borders, xe, xo, ze, zo)
    slot_out.wait()
    send_out.wait()


def parts_of(cells_x):
    step = max(1, cells_x // 8)
    return [(first, min(step, cells_x - first)) for first in range(0, cells_x, step)]


def fetch_fields(fields, sems):
    copies = [[] for _ in fields]
    for n, (first, count) in enumerate(parts_of(fields[0][1].shape[0])):
        planes = pl.ds(first, count)
        for row, (source, target) in enumerate(fields):
            copy = pltpu.make_async_copy(source.at[planes], target.at[planes], sems.at[row, n])
            copy.start()
            copies[row].append(copy)
    return copies


def advect(
    alpha, vx_h, vz_h, p_h, xe_in, xo_in, ze_in, zo_in,
    out_h, early, xe, xo, ze, zo,
    vx, vz, out, p0, p1, pz0, pz1, sems, p_sems,
):
    cells_x, cells_z, beam = alpha.shape
    chunks = cells_z // SUB
    ev_x = even("slab")
    ev_z = even("depth")
    top = row_is((SUB, beam), 0)
    bottom = row_is((SUB, beam), SUB - 1)
    parts = parts_of(cells_x)
    fields = ((vx_h, vx), (vz_h, vz))
    ins = fetch_fields(fields, sems)
    p_ins = fetch(x_planes(p_h) + z_tiles(p_h), [p0, p1, pz0, pz1], p_sems)
    outs = [
        pltpu.make_async_copy(out.at[pl.ds(f, c)], out_h.at[pl.ds(f, c)], sems.at[len(fields), n])
        for n, (f, c) in enumerate(parts)
    ]

    def at(k):
        return pl.ds(k * SUB, SUB)

    has_x, has_z = inner("slab"), inner("depth")

    def plane(x, first, last):
        zlo = has_z[0] * jnp.where(ev_z, zo_in[pl.ds(x, 1), :], ze_in[pl.ds(x, 1), :])
        zhi = has_z[1] * jnp.where(ev_z, ze_in[pl.ds(x, 1), :], zo_in[pl.ds(x, 1), :])
        above = None
        for k in reversed(range(chunks)):
            a = alpha[x, at(k), :]
            v = vx[x, at(k), :]
            if first:
                am = has_x[0] * jnp.where(ev_x, xo_in[at(k), :], xe_in[at(k), :]).astype(F32)
            else:
                am = alpha[x - 1, at(k), :]
            fx = v * jnp.where(v > 0, am, a)
            if last:
                q = has_x[1] * jnp.where(ev_x, xe_in[at(k), :], xo_in[at(k), :]).astype(F32)
                fxn = jnp.where(q > 0, q * a, q)
            else:
                vn = vx[x + 1, at(k), :]
                fxn = vn * jnp.where(vn > 0, a, alpha[x + 1, at(k), :])
            w = vz[x, at(k), :]
            if k == 0:
                edge = jnp.broadcast_to(zlo, a.shape)
            else:
                edge = pltpu.roll(alpha[x, at(k - 1), :], 1, 0)
            ad = jnp.where(top, edge, pltpu.roll(a, 1, 0))
            fz = w * jnp.where(w > 0, ad, a)
            up = pltpu.roll(fz, SUB - 1, 0)
            if above is None:
                q = jnp.broadcast_to(zhi, a.shape)
                fzn = jnp.where(bottom, jnp.where(q > 0, q * a, q), up)
            else:
                fzn = jnp.where(bottom, above, up)
            above = up
            new = a - COURANT * (fxn - fx + fzn - fz)
            out[x, at(k), :] = new
            if k == chunks - 1:
                z_up = new[SUB - 1:SUB, :] - 0.5
            if k == 0:
                z_down = new[0:1, :] - 0.5
        ze[0, pl.ds(x, 1), :] = jnp.where(ev_z, z_up, z_down)
        zo[0, pl.ds(x, 1), :] = jnp.where(ev_z, z_down, z_up)

    for n, (first, count) in enumerate(parts):
        for copies in ins:
            copies[n].wait()
        begin = max(first - 1, 0)
        end = first + count - 1
        if begin == 0:
            plane(0, True, end == begin and cells_x == 1)
            begin = 1

        @pl.loop(begin, end)
        def _(x):
            plane(x, False, False)

        if n == len(parts) - 1:
            plane(cells_x - 1, False, True)
        if n > 0:
            outs[n - 1].start()
    outs[-1].start()
    early[...] = out[pl.ds(0, early.shape[0])]

    for copy in p_ins:
        copy.wait()
    for k in range(chunks):
        for which, up, down in ((0, out[cells_x - 1, at(k), :] - 0.5, out[0, at(k), :] - 0.5), (1, p1[at(k), :], p0[at(k), :])):
            xe[which, at(k), :] = jnp.where(ev_x, up, down).astype(BF16)
            xo[which, at(k), :] = jnp.where(ev_x, down, up).astype(BF16)
    for x in range(cells_x):
        up = pz1[x, SUB - 1:SUB, :]
        down = pz0[x, 0:1, :]
        ze[1, x:x + 1, :] = jnp.where(ev_z, up, down)
        zo[1, x:x + 1, :] = jnp.where(ev_z, down, up)
    for copy in outs:
        copy.wait()


def coefficients(half, cx, cz, cy, inverse, arrived):
    cells_x, cells_z, beam = half.shape
    chunks = cells_z // SUB
    top = row_is((SUB, beam), 0)
    bottom = row_is((SUB, beam), SUB - 1)
    lane = lax.broadcasted_iota(jnp.int32, (SUB, LANES), 1)
    start_lane, end_lane = lane == 0, lane == LANES - 1
    none = jnp.zeros((cells_z, beam), F32)
    cx[0] = none
    cx[cells_x] = none

    def at(k):
        return pl.ds(k * SUB, SUB)

    def first_lane_zero(v):
        return jnp.concatenate([jnp.where(start_lane, 0.0, v[:, :LANES]), v[:, LANES:]], axis=1)

    def plane(x, last):
        above = jnp.zeros((SUB, beam), F32)
        rolled = pltpu.roll(half[x, at(chunks - 1), :], 1, 0)
        for k in reversed(range(chunks)):
            r = half[x, at(k), :]
            total = cx[x, at(k), :]
            if not last:
                hx = 1.0 / (r + half[x + 1, at(k), :])
                cx[x + 1, at(k), :] = hx
                total = total + hx
            if k == 0:
                hz = jnp.where(top, 0.0, 1.0 / (r + rolled))
            else:
                below = pltpu.roll(half[x, at(k - 1), :], 1, 0)
                hz = 1.0 / (r + jnp.where(top, below, rolled))
                rolled = below
            cz[x, at(k), :] = hz
            up = pltpu.roll(hz, SUB - 1, 0)
            total = total + (hz + jnp.where(bottom, above, up))
            above = up
            hy_all = 1.0 / (r + first_lane_zero(pltpu.roll(r, 1, 1)))
            hy = first_lane_zero(hy_all)
            cy[x, at(k), :] = hy
            edge = jnp.where(end_lane, 1.0 / r[:, beam - LANES:], 0.0)
            hy_up = pltpu.roll(hy, beam - 1, 1)
            hy_up = jnp.concatenate(
                [hy_up[:, : beam - LANES], hy_up[:, beam - LANES:] + edge], axis=1
            )
            inverse[x, at(k), :] = 1.0 / (total + (hy_all + hy_up))

    begin = 0
    for stop in arrived():
        @unrolled(begin, stop - 1, 1)
        def _(x):
            plane(x, False)

        begin = stop - 1
    plane(cells_x - 1, True)


def close(
    p_in, inverse_in, half, xe_in, xo_in, ze_in, zo_in,
    p, inverse, gx, gz, xe, xo, ze, zo,
    wx,
):
    del p_in, inverse_in
    cells_x, cells_z, beam = half.shape
    chunks = cells_z // SUB
    ev_x, ev_z = even("slab"), even("depth")
    has = [inner("slab"), inner("depth")]

    def at(k):
        return pl.ds(k * SUB, SUB)

    for side, x in ((0, 0), (1, cells_x - 1)):
        for k in range(chunks):
            a, b = xe_in[:, at(k), :], xo_in[:, at(k), :]
            v = (jnp.where(ev_x, a, b) if side else jnp.where(ev_x, b, a)).astype(F32)
            halo = has[0][side] * (4.5 * v[0] + 2.75)
            c = 1.0 / (half[x, at(k), :] + halo)
            w = 1.0 / inverse[x, at(k), :]
            open_c = has[0][side] * c
            p[x, at(k), :] = p[x, at(k), :] * w + open_c * v[1]
            gx[side, at(k), :] = open_c
            wx[side, at(k), :] = w + c

    def rows(x, plane):
        faces = []
        for side, k in ((0, 0), (1, chunks - 1)):
            here = row_is((SUB, beam), 0 if side == 0 else SUB - 1)
            a, b = ze_in[:, pl.ds(x, 1), :], zo_in[:, pl.ds(x, 1), :]
            v = jnp.where(ev_z, a, b) if side else jnp.where(ev_z, b, a)
            halo = jnp.broadcast_to(has[1][side] * (4.5 * v[0] + 2.75), (SUB, beam))
            c = jnp.where(here, 1.0 / (half[x, at(k), :] + halo), 0.0)
            open_c = has[1][side] * c
            add = open_c * jnp.broadcast_to(v[1], (SUB, beam))
            if plane is None:
                w = 1.0 / inverse[x, at(k), :]
                total = p[x, at(k), :] * w + add
                inv = 1.0 / (w + c)
                inverse[x, at(k), :] = inv
                new = total * inv
                p[x, at(k), :] = new
            else:
                w = wx[plane, at(k), :] + c
                wx[plane, at(k), :] = w
                inv = 1.0 / w
                total = p[x, at(k), :] + add
                p[x, at(k), :] = total
                new = total * inv
            g = inv * open_c
            r = slice(0, 1) if side == 0 else slice(SUB - 1, SUB)
            gz[side, pl.ds(x, 1), :] = g[r, :]
            faces.append(new[r, :])
        ze[pl.ds(x, 1), :] = jnp.where(ev_z, faces[1], faces[0])
        zo[pl.ds(x, 1), :] = jnp.where(ev_z, faces[0], faces[1])

    rows(0, 0)
    rows(cells_x - 1, 1)

    @unrolled(1, cells_x - 1)
    def _(x):
        rows(x, None)

    for k in range(chunks):
        new = []
        for side, x in ((0, 0), (1, cells_x - 1)):
            inv = 1.0 / wx[side, at(k), :]
            inverse[x, at(k), :] = inv
            gx[side, at(k), :] = gx[side, at(k), :] * inv
            new.append(p[x, at(k), :] * inv)
            p[x, at(k), :] = new[side]
        xe[at(k), :] = jnp.where(ev_x, new[1], new[0]).astype(BF16)
        xo[at(k), :] = jnp.where(ev_x, new[0], new[1]).astype(BF16)


def by_lanes(ref):
    _, _, beam = ref.shape
    blocks = beam // LANES
    for b in range(blocks):
        yield b, pl.ds(b * LANES, LANES)


def middle(
    capacity, rows, got, early, alpha_h, div_h, p_h,
    half, cx, cz, cy, inverse, rhs, p, row_out,
    hull, div, p0, rec32, row_v, row_s, sems, sem,
):
    devices = got.shape[0] // rows
    cells_x, cells_z, beam = rhs.shape
    blocks = beam // LANES
    rec32[...] = got[...].astype(F32)
    digits = rec32[pl.ds(rows - 1, devices, stride=rows), :]
    seg = (digits * float(DIGIT) + pltpu.roll(digits, LANES - capacity, 1)).astype(jnp.int32) - DIGIT
    across = seg // blocks
    row = ((across // cells_z) * blocks + seg % blocks) * cells_z + across % cells_z
    slots = lax.broadcasted_iota(jnp.int32, seg.shape, 0) * capacity
    slots = slots + lax.broadcasted_iota(jnp.int32, seg.shape, 1)
    row = jnp.where(seg < 0, slots % hull.shape[0], row)
    row_v[...] = row
    copy = pltpu.make_async_copy(row_v, row_s, sem)
    copy.start()
    per = LANES // capacity
    lane = lax.broadcasted_iota(jnp.int32, (devices // per, LANES), 1)
    table = jnp.zeros(lane.shape, jnp.int32)
    for j in range(per):
        piece = pltpu.roll(row_v[pl.ds(j, devices // per, stride=per), :], j * capacity, 1)
        table = jnp.where(lane // capacity == j, piece, table)
    row_out[pl.ds(0, devices // per)] = table
    cut = early.shape[0]
    late = pl.ds(cut, cells_x - cut)
    alpha_in = pltpu.make_async_copy(alpha_h.at[late], half.at[late], sems.at[0])
    alpha_in.start()
    rest = [
        pltpu.make_async_copy(h, v, sems.at[1 + n]) for n, (h, v) in enumerate(((div_h, div), (p_h, p0)))
    ]
    for other in rest:
        other.start()

    def arrived():
        half[pl.ds(0, cut)] = 0.5 + 4.5 * early[...]
        yield cut
        hull[...] = jnp.zeros_like(hull)
        alpha_in.wait()

        @unrolled(cut, cells_x)
        def _(x):
            half[x] = 0.5 + 4.5 * half[x]

        yield cells_x

    coefficients(half, cx, cz, cy, inverse, arrived)
    copy.wait()

    @pl.loop(0, devices)
    def _(d):
        for s in range(capacity):
            hull[pl.ds(row_s[d, s], 1), :] += rec32[pl.ds(d * rows + s, 1), :]

    for other in rest:
        other.wait()

    def source(x, at):
        parts = []
        for b, lanes in by_lanes(rhs):
            first = pl.multiple_of((x * blocks + b) * cells_z + at.start, SUB)
            parts.append(div[x, at, lanes] + hull[pl.ds(first, SUB), :])
        value = jnp.concatenate(parts, axis=1)
        rhs[x, at, :] = value
        return value

    sweep(p0, cx, cz, cy, inverse, source, p)


def sweep(p, cx, cz, cy, inverse, source, out, start=0, stop=None):
    cells_x, cells_z, beam = p.shape
    chunks = cells_z // SUB
    top = row_is((SUB, beam), 0)
    bottom = row_is((SUB, beam), SUB - 1)

    def at(k):
        return pl.ds(k * SUB, SUB)

    @unrolled(start, cells_x if stop is None else stop)
    def _(x):
        prv = jnp.maximum(x - 1, 0)
        nxt = jnp.minimum(x + 1, cells_x - 1)
        above = jnp.zeros((SUB, beam), F32)
        rolled = pltpu.roll(p[x, at(chunks - 1), :], 1, 0)
        for k in reversed(range(chunks)):
            here = p[x, at(k), :]
            hz = cz[x, at(k), :]
            hy = cy[x, at(k), :]
            total = cx[x, at(k), :] * p[prv, at(k), :] + cx[x + 1, at(k), :] * p[nxt, at(k), :]
            if k > 0:
                below = pltpu.roll(p[x, at(k - 1), :], 1, 0)
                down = jnp.where(top, below, rolled)
                rolled = below
            else:
                down = rolled
            up = pltpu.roll(hz * here, SUB - 1, 0)
            total = total + (hz * down + jnp.where(bottom, above, up))
            above = up
            total = total + (hy * pltpu.roll(here, 1, 1) + pltpu.roll(hy * here, beam - 1, 1))
            out[x, at(k), :] = (total - source(x, at(k))) * inverse[x, at(k), :]


def next_sweep(p, cx, cz, cy, inverse, rhs, out):
    sweep(p, cx, cz, cy, inverse, lambda x, at: rhs[x, at, :], out)


def add_borders(p_in, xe_in, xo_in, ze_in, zo_in, gx, gz, p, send=None):
    del p_in
    cells_x, cells_z, beam = p.shape
    chunks = cells_z // SUB
    ev_x, ev_z = even("slab"), even("depth")

    def at(k):
        return pl.ds(k * SUB, SUB)

    for side, x in ((0, 0), (1, cells_x - 1)):
        for k in range(chunks):
            a, b = xe_in[at(k), :], xo_in[at(k), :]
            v = jnp.where(ev_x, a, b) if side else jnp.where(ev_x, b, a)
            p[x, at(k), :] = p[x, at(k), :] + gx[side, at(k), :] * v.astype(F32)

    @unrolled(0, cells_x)
    def _(x):
        faces = []
        for side, k in ((0, 0), (1, chunks - 1)):
            here = row_is((SUB, beam), 0 if side == 0 else SUB - 1)
            a, b = ze_in[pl.ds(x, 1), :], zo_in[pl.ds(x, 1), :]
            v = jnp.where(ev_z, a, b) if side else jnp.where(ev_z, b, a)
            add = jnp.broadcast_to(gz[side, pl.ds(x, 1), :] * v, (SUB, beam))
            new = p[x, at(k), :] + jnp.where(here, add, 0.0)
            p[x, at(k), :] = new
            faces.append(new[0:1, :] if side == 0 else new[SUB - 1:SUB, :])
        if send is not None:
            send[2][pl.ds(x, 1), :] = jnp.where(ev_z, faces[1], faces[0])
            send[3][pl.ds(x, 1), :] = jnp.where(ev_z, faces[0], faces[1])

    if send is not None:
        for k in range(chunks):
            lo, hi = p[0, at(k), :], p[cells_x - 1, at(k), :]
            send[0][at(k), :] = jnp.where(ev_x, hi, lo).astype(BF16)
            send[1][at(k), :] = jnp.where(ev_x, lo, hi).astype(BF16)


def fix_and_send(p_in, xe_in, xo_in, ze_in, zo_in, gx, gz, p, xe, xo, ze, zo):
    add_borders(p_in, xe_in, xo_in, ze_in, zo_in, gx, gz, p, (xe, xo, ze, zo))


def inner_part(ref, count):
    return ref.at[pl.ds(1, count), pl.ds(SUB, ref.shape[1] - 2 * SUB), :]


def border_parts(ref, count):
    cells_x, cells_z, _ = ref.shape
    planes = pl.ds(1, count)
    return [
        ref.at[0],
        ref.at[pl.ds(count + 1, cells_x - count - 1)],
        ref.at[planes, pl.ds(0, SUB), :],
        ref.at[planes, pl.ds(cells_z - SUB, SUB), :],
    ]


def early_planes(cells_x):
    return max(1, cells_x // 2 - 1)


def last_sweep(p, cx, cz, cy, inverse, rhs, out, out_h, sem):
    count = early_planes(p.shape[0])
    copy = pltpu.make_async_copy(inner_part(out, count), inner_part(out_h, count), sem)
    sweep(p, cx, cz, cy, inverse, lambda x, at: rhs[x, at, :], out, stop=count + 1)
    copy.start()
    sweep(p, cx, cz, cy, inverse, lambda x, at: rhs[x, at, :], out, start=count + 1)
    copy.wait()


def fix_and_gather(
    p_in, xe_in, xo_in, ze_in, zo_in, gx, gz, row_v, out_in, p, back, out_h, split, rows32, row, sem, sems
):
    del out_in
    cells_x, cells_z, beam = p.shape
    row_copy = pltpu.make_async_copy(row_v.at[pl.ds(0, row.shape[0])], row, sem)
    row_copy.start()
    add_borders(p_in, xe_in, xo_in, ze_in, zo_in, gx, gz, p)
    count = early_planes(cells_x)
    outs = fetch(border_parts(p, count), border_parts(out_h, count), sems)
    blocks = beam // LANES

    @unrolled(0, cells_x)
    def _(x):
        for b, lanes in by_lanes(p):
            first = pl.multiple_of((x * blocks + b) * cells_z, SUB)
            split[pl.ds(first, cells_z), :] = p[x, :, lanes]

    row_copy.wait()

    @pl.loop(0, row.shape[0])
    def _(g):
        for lane in range(LANES):
            rows32[pl.ds(g * LANES + lane, 1), :] = split[pl.ds(row[g, lane], 1), :]

    back[...] = rows32[...].astype(BF16).reshape(back.shape)
    for copy in outs:
        copy.wait()


def leave(back, slot, out):
    rows = back.shape[0] * back.shape[1]
    panels = out.shape[0]
    pick = lax.broadcasted_iota(jnp.int32, (rows, panels), 0) == slot[...]
    out[...] = lax.dot_general(
        jnp.where(pick, 1.0, 0.0).astype(BF16),
        back[...].reshape(rows, LANES),
        (((0,), (0,)), ((), ())),
        preferred_element_type=F32,
    ).astype(BF16)


def body(alpha, vel_x, vel_z, divergence, press_guess, panel_records, panel_dest, panel_segment):
    devices = lax.axis_size("slab") * lax.axis_size("depth")
    panels = panel_records.shape[0]
    capacity = 2 * panels // devices
    cells_x, cells_z, beam = alpha.shape
    field = shape(alpha.shape)
    rows = (capacity + 2) // 2 * 2
    axes = ("slab", "depth")

    xs, zs = (cells_z, beam), (cells_x, beam)
    tile = (cells_x, SUB, beam)
    faces = [shape(xs, BF16)] * 2 + [shape(zs)] * 2
    two_faces = [shape((2,) + xs, BF16)] * 2 + [shape((2,) + zs)] * 2
    parts = len(parts_of(cells_x))
    table = (devices * capacity // LANES, LANES)
    lines = (cells_x * cells_z * beam // LANES, LANES)

    def near(dims, dtype=F32):
        return pltpu.VMEM(tuple(dims), dtype)

    def swaps(xe, xo, ze, zo):
        return swap(xe, "slab", 0), swap(xo, "slab", 1), swap(ze, "depth", 0), swap(zo, "depth", 1)

    *packed, send, slot = call(
        functools.partial(enter, capacity, rows, devices),
        faces + [shape((devices * rows, LANES), BF16), shape((1, panels), jnp.int32)],
        alpha, vel_x, vel_z,
        panel_dest.reshape(1, panels), panel_segment.reshape(1, panels), panel_records,
        far_in=(0, 1, 2, 3, 4, 5), far_out=(4, 5),
        scratch=[
            near(xs), near(xs), near(tile), near(tile), near(xs), near(tile),
            near((1, panels), jnp.int32),
            near((1, panels), jnp.int32),
            near((panels, LANES), BF16),
            near((1, panels), jnp.int32),
            near((devices * rows, LANES), BF16),
            DMA((11,)),
        ],
    )
    halo = swaps(*packed)
    got = lax.all_to_all(
        send.reshape(devices, rows // 2, 2, LANES), axes, split_axis=0, concat_axis=0, tiled=True
    ).reshape(devices * rows, LANES)
    cut = max(1, cells_x // 4)
    alpha_next, early, *packed = call(
        advect, [field, shape((cut,) + xs)] + two_faces, alpha, vel_x, vel_z, press_guess, *halo,
        far_in=(1, 2, 3), far_out=(0,),
        scratch=[near(alpha.shape)] * 3 + [near(xs), near(xs), near(tile), near(tile), DMA((4, parts)), DMA((4,))],
    )
    halo = swaps(*packed)
    half, cx, cz, cy, inverse, rhs, pressure, row = call(
        functools.partial(middle, capacity, rows),
        [field, shape((cells_x + 1,) + xs), field, field, field, field, field, shape((devices, LANES), jnp.int32)],
        got, early, alpha_next, divergence, press_guess,
        far_in=(2, 3, 4),
        scratch=[
            near(lines),
            near(alpha.shape),
            near(alpha.shape),
            near((devices * rows, LANES)),
            near((devices, LANES), jnp.int32),
            pltpu.SMEM((devices, LANES), jnp.int32),
            DMA((3,)),
            DMA,
        ],
    )
    pressure, inverse, gx, gz, *packed = call(
        close,
        [field, field, shape((2,) + xs), shape((2,) + zs)] + faces,
        pressure, inverse, half, *halo,
        aliases={0: 0, 1: 1},
        scratch=[near((2,) + xs)],
    )
    halo = swaps(*packed)
    (pressure,) = call(next_sweep, [field], pressure, cx, cz, cy, inverse, rhs)
    pressure, *packed = call(fix_and_send, [field] + faces, pressure, *halo, gx, gz, aliases={0: 0})
    halo = swaps(*packed)
    last, out = call(last_sweep, [field, field], pressure, cx, cz, cy, inverse, rhs, far_out=(1,), scratch=[DMA])
    _, back, pressure = call(
        fix_and_gather,
        [field, shape((devices, capacity, LANES), BF16), field],
        last, *halo, gx, gz, row, out,
        far_in=(8,), far_out=(2,),
        aliases={0: 0, 8: 2},
        scratch=[
            near(lines),
            near((devices * capacity, LANES)),
            pltpu.SMEM(table, jnp.int32),
            DMA,
            DMA((4,)),
        ],
    )
    returned = lax.all_to_all(back, axes, split_axis=0, concat_axis=0, tiled=True)
    (panel_pressure,) = call(leave, [shape((panels, LANES), BF16)], returned, slot, free_out=(0,), limit=4 * MIB)
    return (pressure, alpha_next, panel_pressure)


def solution(mesh):
    in_specs = (
        P("slab", "depth", None),
        P("slab", "depth", None),
        P("slab", "depth", None),
        P("slab", "depth", None),
        P("slab", "depth", None),
        P(("slab", "depth"), None),
        P(("slab", "depth"), None),
        P(("slab", "depth"), None),
    )
    out_specs = (P("slab", "depth", None), P("slab", "depth", None), P(("slab", "depth"), None))
    return jax.shard_map(body, mesh=mesh, in_specs=in_specs, out_specs=out_specs, check_vma=False)
```
